32 devices in a mesh: groups: 2 (over y), seq: 4 (over z), tp: 4 (over x, core).
Axes of the slice: x: 2, y: 2, z: 4, core: 2. Of those that a mesh axis runs over, the one named last changes fastest.
Arguments:
- queries: bfloat16 [8, 128, 5120], P('groups', 'seq', 'tp'), parts along dimension 0, may hold values from -40 to 40
- key_vectors: bfloat16 [8, 128, 5120], P('groups', 'seq', 'tp'), parts along dimension 0, may hold values from -40 to 40
- value_vectors: bfloat16 [8, 128, 5120], P('groups', 'seq', 'tp'), parts along dimension 0, may hold values from -6 to 6
- block_mask: int32 [40, 4, 4], P('tp'), may hold values from 0 to 1, as said below
- out_weight: bfloat16 [40, 128, 2560], P('tp', 'seq'), may hold values from -0.5 to 0.5
Outputs:
- projected: bfloat16 [8, 128, 2560], P('groups', 'seq', 'tp'), parts along dimension 0
The draws below stay inside these ranges and needn't reach their ends.
There are 2 independent parts, one for each index of `groups`. The reference program is written for one: setup_inputs(seed, part) draws one part's arguments, and reference() takes and returns one part's arrays. A program takes and returns all parts, laid end to end along the dimension named above; an argument that names none is the same for every part. Nothing has to cross between parts.
Inputs may be any that keep to these rules, and one draw needn't show every extreme that they name: block_mask[h, b, b] = 1 for every head and block; every row of a head's mask has at most 4 ones, and every head has a row with exactly 4.
All inputs are finite; a program needn't handle non-finite values.
Results may differ from the reference program's by a relative error of at most 0.012.
Values may be sent and summed in bfloat16 or wider, within the bound.
No kernel may reach another device: no remote copies, remote signals or barrier semaphores. Data moves between devices by JAX's collectives and lax.ppermute only.
A program may use at most 64 MiB of HBM per device.

```python
import jax
import jax.numpy as jnp
from jax import lax

HEADS = 40
HD = 128
DOUT = 2560
BLOCK = 128
NB = 4
KMAX = 4


def query_key_pair(key):
    base = jax.random.fold_in(key, 11)
    first_key, second_key = jax.random.split(base)
    shape = (NB, BLOCK, HEADS * HD)
    spread = 2.0 ** 0.5
    query_raw = jnp.clip(jax.random.normal(first_key, shape, jnp.float32) * spread, -6.0 * spread, 6.0 * spread)
    key_raw = jnp.clip(jax.random.normal(second_key, shape, jnp.float32) * spread, -6.0 * spread, 6.0 * spread)
    return (query_raw, key_raw)


def draw_queries(key, part):
    query_raw, key_raw = query_key_pair(key)
    return query_raw.astype(jnp.bfloat16)


def draw_key_vectors(key, part):
    query_raw, key_raw = query_key_pair(key)
    return key_raw.astype(jnp.bfloat16)


def draw_block_mask(key, part):
    first_key, second_key, third_key, fourth_key = jax.random.split(jax.random.fold_in(key, 23), 4)
    lowest = jax.random.randint(first_key, (HEADS, 1), 1, KMAX + 1)
    uniform_bits = jax.random.randint(second_key, (HEADS, NB), 0, 1 << 20)
    wanted = lowest + uniform_bits % (KMAX - lowest + 1)
    forced_row = jax.random.randint(fourth_key, (HEADS, 1), 0, NB)
    row_ids = jnp.arange(NB, dtype=jnp.int32)
    wanted = jnp.where(row_ids[None, :] == forced_row, KMAX, wanted)
    noise = jax.random.randint(third_key, (HEADS, NB, NB), 0, 1 << 20)
    ranking = noise * NB + row_ids[None, None, :]
    diagonal = row_ids[:, None] == row_ids[None, :]
    ranking = jnp.where(diagonal[None, :, :], -1, ranking)
    position = jnp.argsort(jnp.argsort(ranking, axis=-1), axis=-1)
    return (position < wanted[:, :, None]).astype(jnp.int32)


def shard_levels(stream_key, extent, shards, smallest, high):
    gain = 1.0
    for dim, blocks in shards:
        draws = jax.random.uniform(jax.random.fold_in(jax.random.fold_in(stream_key, 6), dim), (blocks,), jnp.float32, smallest / len(shards), high / len(shards))
        gain = gain * jnp.repeat(jnp.exp(draws), extent[dim] // blocks).reshape((-1,) + (1,) * (len(extent) - 1 - dim))
    return gain


def normal_values(own_key, shape, width, most, cuts=(), kind=jnp.bfloat16):
    result = jax.random.normal(own_key, shape, jnp.float32) * width
    if len(cuts) > 0:
        result = shard_levels(own_key, shape, cuts, -0.22, 0.18) * result
    return jnp.clip(result, min=-most, max=most).astype(kind)


def setup_inputs(seed: int = 0, part: int = 0) -> dict:
    streams_of = jax.random.split(jax.random.key(seed), 6)
    own_keys = jax.random.split(jax.random.fold_in(streams_of[5], part), 6)
    return {
        "queries": draw_queries(jax.random.fold_in(jax.random.fold_in(streams_of[5], part), 71), part),
        "key_vectors": draw_key_vectors(jax.random.fold_in(jax.random.fold_in(streams_of[5], part), 71), part),
        "value_vectors": normal_values(own_keys[2], (NB, BLOCK, HEADS * HD), 1.0, 6.0, ((1, 4), (2, 4))),
        "block_mask": draw_block_mask(jax.random.fold_in(streams_of[5], 71), part),
        "out_weight": normal_values(streams_of[4], (HEADS, HD, DOUT), HD ** -0.5, 0.5, ((0, 4), (1, 4))),
    }


def attend_head(head_queries, head_keys, head_values, head_mask):
    column_ids = jnp.arange(NB, dtype=jnp.int32)
    ranking = (1 - head_mask) * NB + column_ids[None, :]
    key_pick = jnp.argsort(ranking, axis=-1)[:, :KMAX].astype(jnp.int32)
    key_live = jnp.take_along_axis(head_mask, key_pick, axis=-1)
    chosen_keys = head_keys[key_pick].astype(jnp.float32)
    chosen_values = head_values[key_pick].astype(jnp.float32)
    scores = jnp.einsum("qid,qkjd->qikj", head_queries.astype(jnp.float32), chosen_keys) * (HD ** -0.5)
    scores = jnp.where((key_live > 0)[:, None, :, None], scores, -jnp.inf)
    largest = jnp.max(scores, axis=(2, 3), keepdims=True)
    weights = jnp.exp(scores - largest)
    totals = jnp.sum(weights, axis=(2, 3))
    rounded = lax.optimization_barrier(weights.astype(jnp.bfloat16)).astype(jnp.float32)
    blended = jnp.einsum("qikj,qkjd->qid", rounded, chosen_values)
    return (blended / totals[..., None]).astype(jnp.bfloat16)


def reference(queries, key_vectors, value_vectors, block_mask, out_weight):
    def one_head(head_index):
        start_col = (head_index * HD).astype(jnp.int32)
        head_queries = lax.dynamic_slice_in_dim(queries, start_col, HD, 2)
        head_keys = lax.dynamic_slice_in_dim(key_vectors, start_col, HD, 2)
        head_values = lax.dynamic_slice_in_dim(value_vectors, start_col, HD, 2)
        return attend_head(head_queries, head_keys, head_values, block_mask[head_index])

    per_head = lax.map(one_head, jnp.arange(HEADS, dtype=jnp.int32))
    joined = per_head.transpose(1, 2, 0, 3).reshape(NB * BLOCK, HEADS * HD)
    product = jnp.dot(joined, out_weight.reshape(HEADS * HD, DOUT), preferred_element_type=jnp.float32)
    return product.astype(jnp.bfloat16).reshape(NB, BLOCK, DOUT)
```

```python
import functools

import jax
import jax.numpy as jnp
import numpy as np
from jax import lax
from jax.experimental import pallas as pl
from jax.experimental.pallas import tpu as pltpu
from jax.sharding import PartitionSpec as P

KEYS = 28


def strip_tables(heads_local, blocks, slot_total):
    slot_ids = np.arange(slot_total)
    head_of = slot_ids * heads_local // slot_total
    per_head = np.bincount(head_of, minlength=heads_local)
    head_begin = np.cumsum(per_head) - per_head
    order_in_head = slot_ids - head_begin[head_of]
    head_share = per_head[head_of]
    first_block = order_in_head * blocks // head_share
    block_count = (order_in_head + 1) * blocks // head_share - first_block
    return (head_of, first_block, block_count)


def gathered_plan(queries, key_vectors, value_vectors, block_mask, out_weight):
    rank_count = lax.axis_size("seq")
    my_rank = lax.axis_index("seq")
    block_total, row_share, feature_width = queries.shape
    heads_local = block_mask.shape[0]
    head_size = feature_width // heads_local
    block_rows = row_share * rank_count
    per_rank = (heads_local + rank_count - 1) // rank_count
    slot_total = rank_count * per_rank
    least_share = slot_total // heads_local
    strip_cap = ((block_total + least_share - 1) // least_share + 1) // 2 * 2
    key_cap = min(KEYS, block_total)
    head_of, first_block, block_count = strip_tables(heads_local, block_total, slot_total)
    slot_grid = np.arange(slot_total).reshape(rank_count, per_rank).T
    paired = jnp.concatenate(
        [
            key_vectors.reshape(block_total, row_share, heads_local, head_size),
            value_vectors.reshape(block_total, row_share, heads_local, head_size),
        ],
        axis=3,
    )
    send_heads = jnp.asarray(head_of[slot_grid].reshape(-1), jnp.int32)
    chosen = jnp.take(paired, send_heads, axis=2)
    chosen = chosen.reshape(block_total, row_share, per_rank, rank_count, 2 * head_size)
    outgoing_pairs = chosen.transpose(2, 0, 3, 1, 4).reshape(
        per_rank, block_total, block_rows, 2 * head_size
    )
    flat_queries = queries.reshape(block_total, row_share, heads_local, head_size).transpose(
        0, 2, 1, 3
    )
    flat_queries = flat_queries.reshape(block_total * heads_local, row_share, head_size)
    positions = np.arange(strip_cap)
    unit_block = first_block[slot_grid][:, None, :] + positions[None, :, None]
    is_live = positions[None, :, None] < block_count[slot_grid][:, None, :]
    unit_index = np.where(is_live, unit_block * heads_local + head_of[slot_grid][:, None, :], 0)
    picked = jnp.take(flat_queries, jnp.asarray(unit_index.reshape(-1), jnp.int32), axis=0)
    picked = jnp.where(
        jnp.asarray(is_live.reshape(-1))[:, None, None], picked, jnp.zeros_like(picked)
    )
    outgoing_queries = picked.reshape(per_rank, strip_cap, block_rows, head_size)
    strip_queries, strip_pairs = (
        lax.all_to_all(outgoing_queries, "seq", split_axis=2, concat_axis=2, tiled=True),
        lax.all_to_all(outgoing_pairs, "seq", split_axis=2, concat_axis=2, tiled=True),
    )
    my_slots = my_rank * per_rank + jnp.arange(per_rank, dtype=jnp.int32)
    my_heads = jnp.asarray(head_of, jnp.int32)[my_slots]
    my_first = jnp.asarray(first_block, jnp.int32)[my_slots]
    query_blocks = jnp.minimum(
        my_first[:, None] + jnp.arange(strip_cap, dtype=jnp.int32)[None, :], block_total - 1
    )
    mask_rows = block_mask[my_heads[:, None], query_blocks]
    column_ids = jnp.arange(block_total, dtype=jnp.int32)
    ranking = (1 - mask_rows) * block_total + column_ids
    key_pick = jnp.argsort(ranking, axis=-1)[..., :key_cap]
    key_live = jnp.take_along_axis(mask_rows, key_pick, axis=-1)
    group_total = per_rank * strip_cap // 2
    query_groups = strip_queries.reshape(group_total, 2, block_rows, head_size)
    pick_groups = key_pick.reshape(group_total, 2, key_cap)
    live_groups = key_live.reshape(group_total, 2, key_cap)
    slot_of_group = jnp.arange(group_total, dtype=jnp.int32) // (strip_cap // 2)
    score_scale = head_size ** (-0.5)

    def attend_group(inputs):
        query_tile, pick_tile, live_tile, slot_index = inputs
        pairs_here = strip_pairs[slot_index]
        gathered = pairs_here[pick_tile]
        scores = (
            jnp.einsum(
                "qid,qkjd->qikj",
                query_tile,
                gathered[..., :head_size],
                preferred_element_type=jnp.float32,
            )
            * score_scale
        )
        allowed = (live_tile > 0)[:, None, :, None]
        scores = jnp.where(allowed, scores, -jnp.inf)
        largest = jnp.max(scores, axis=(2, 3), keepdims=True)
        weights = jnp.exp(scores - largest)
        totals = jnp.sum(weights, axis=(2, 3))
        blended = jnp.einsum(
            "qikj,qkjd->qid",
            weights.astype(jnp.bfloat16),
            gathered[..., head_size:],
            preferred_element_type=jnp.float32,
        )
        return (blended / totals[..., None]).astype(jnp.bfloat16)

    strip_out = lax.map(attend_group, (query_groups, pick_groups, live_groups, slot_of_group))
    outgoing_out = strip_out.reshape(per_rank, strip_cap, block_rows, head_size)
    returned = lax.all_to_all(outgoing_out, "seq", split_axis=2, concat_axis=2, tiled=True)
    slot_mesh, step_mesh = np.meshgrid(np.arange(slot_total), positions, indexing="ij")
    live_slot = step_mesh < block_count[slot_mesh]
    placement_index = np.zeros((block_total, heads_local), np.int64)
    source_index = (
        slot_mesh % per_rank * strip_cap + step_mesh
    ) * rank_count + slot_mesh // per_rank
    placement_index[
        first_block[slot_mesh][live_slot] + step_mesh[live_slot], head_of[slot_mesh][live_slot]
    ] = source_index[live_slot]
    flat_back = returned.reshape(per_rank * strip_cap * rank_count, row_share, head_size)
    own_out = jnp.take(flat_back, jnp.asarray(placement_index.reshape(-1), jnp.int32), axis=0)
    own_out = own_out.reshape(block_total, heads_local, row_share, head_size)
    token_total = block_total * row_share
    token_out = own_out.transpose(0, 2, 1, 3).reshape(token_total, heads_local, head_size)
    partial_sum = jnp.einsum(
        "thd,hdo->to",
        token_out,
        lax.all_gather(out_weight, "seq", axis=1, tiled=True),
        preferred_element_type=jnp.float32,
    )
    summed = lax.psum_scatter(
        partial_sum.astype(jnp.bfloat16), "tp", scatter_dimension=1, tiled=True
    ).astype(jnp.float32)
    return summed.astype(jnp.bfloat16).reshape(block_total, row_share, summed.shape[1])


def exchange(array, axis, flip):
    size = lax.axis_size(axis)
    return lax.ppermute(array, axis, [(i, i ^ flip) for i in range(size)])


def aligned(index, unit):
    return pl.multiple_of(index * unit, unit)


class Sizes:
    def __init__(self, rank_count, tp_count, queries_shape, heads_local, weight_shape):
        self.ranks = rank_count
        self.tps = tp_count
        self.blocks, self.rows, width = queries_shape
        self.heads = heads_local
        self.hd = width // heads_local
        self.whole = heads_local // rank_count
        self.rest = heads_local % rank_count
        self.sharers = rank_count // self.rest if self.rest else 1
        self.strip = self.blocks // self.sharers if self.rest else 0
        self.slots = self.whole + (1 if self.rest else 0)
        self.q_units = self.whole * self.blocks + self.strip
        self.kv_units = self.slots * self.blocks
        self.units = self.q_units + 2 * self.kv_units
        self.block_rows = self.rows * rank_count
        self.tokens = self.blocks * self.block_rows
        self.out_tokens = self.q_units * self.block_rows
        self.part = weight_shape[1]
        self.dout = weight_shape[2]
        self.cols = self.dout // tp_count

    def fits(self):
        power = lambda n: n & (n - 1) == 0
        if not (power(self.ranks) and power(self.tps) and self.whole > 0):
            return False
        if self.rest and (self.ranks % self.rest or self.blocks % self.sharers):
            return False
        if self.rows % 32 or self.part % 32 or self.hd % 128 or self.cols % 128:
            return False
        gathered = (self.ranks - 1) * self.heads * self.part * self.dout
        summed = (self.ranks - 1) * self.tokens // self.ranks * self.cols
        summed += (self.tps - 1) * self.heads * self.part * (self.cols + self.tokens)
        return summed < gathered


def pack_kernel(z, q_ref, k_ref, v_ref, *out_refs):
    me = lax.axis_index("seq")
    for flip in range(z.ranks):
        peer = me ^ flip
        out = out_refs[flip]
        for slot in range(z.whole):
            cols = pl.ds(aligned(slot * z.ranks + peer, z.hd), z.hd)
            at = slot * z.blocks
            out[at : at + z.blocks] = q_ref[:, :, cols]
            at += z.q_units
            out[at : at + z.blocks] = k_ref[:, :, cols]
            at += z.kv_units
            out[at : at + z.blocks] = v_ref[:, :, cols]
        if z.rest:
            head = z.whole * z.ranks + peer // z.sharers
            cols = pl.ds(aligned(head, z.hd), z.hd)
            first = (peer % z.sharers) * z.strip
            at = z.whole * z.blocks
            out[at : at + z.strip] = q_ref[pl.ds(first, z.strip), :, cols]
            at += z.q_units
            out[at : at + z.blocks] = k_ref[:, :, cols]
            at += z.kv_units
            out[at : at + z.blocks] = v_ref[:, :, cols]


def weight_kernel(z, w_ref, *out_refs):
    me = lax.axis_index("tp")
    for flip in range(z.tps):
        out_refs[flip][...] = w_ref[:, :, pl.ds(aligned(me ^ flip, z.cols), z.cols)]


def attend_kernel(z, mask_ref, *refs):
    part_refs = refs[: z.ranks]
    out_refs = refs[z.ranks : 2 * z.ranks]
    query, keys, values, weights, result = refs[2 * z.ranks :]
    me = lax.axis_index("seq")
    scale = z.hd ** (-0.5)
    for slot in range(z.slots):
        is_strip = slot >= z.whole
        count = z.strip if is_strip else z.blocks
        head = z.whole * z.ranks + me // z.sharers if is_strip else slot * z.ranks + me
        first = (me % z.sharers) * z.strip if is_strip else 0
        for flip in range(z.ranks):
            source = me ^ flip
            for b in range(count):
                rows = pl.ds(b * z.block_rows + aligned(source, z.rows), z.rows)
                query[slot, rows, :] = part_refs[flip][slot * z.blocks + b]
            for b in range(z.blocks):
                rows = pl.ds(b * z.block_rows + flip * z.rows, z.rows)
                unit = z.q_units + slot * z.blocks + b
                keys[slot, rows, :] = part_refs[flip][unit]
                values[slot, rows, :] = part_refs[flip][unit + z.kv_units]
        wide = count * z.block_rows
        inverses = []
        for b in range(count):
            lanes = slice(b * z.block_rows, (b + 1) * z.block_rows)
            scores = (
                lax.dot_general(
                    keys[slot],
                    query[slot, lanes, :],
                    (((1,), (1,)), ((), ())),
                    preferred_element_type=jnp.float32,
                )
                * scale
            )
            tiles = []
            for t in range(z.blocks):
                tile = scores[t * z.block_rows : (t + 1) * z.block_rows]
                tiles.append(jnp.where(mask_ref[head, first + b, t] > 0, tile, -jnp.inf))
            scores = jnp.concatenate(tiles, axis=0)
            largest = jnp.max(scores, axis=0, keepdims=True)
            exps = jnp.exp(scores - largest)
            inverses.append(jnp.sum(exps, axis=0, keepdims=True))
            weights[:, lanes] = exps.astype(jnp.bfloat16)
        blended = lax.dot_general(
            values[slot],
            weights[:, :wide],
            (((0,), (0,)), ((), ())),
            preferred_element_type=jnp.float32,
        )
        blended = blended / jnp.concatenate(inverses, axis=1)
        lanes = slice(slot * z.tokens, slot * z.tokens + wide)
        result[:, lanes] = blended.astype(jnp.bfloat16)
    for flip in range(z.ranks):
        out_refs[flip][...] = result[pl.ds(aligned(me ^ flip, z.part), z.part), :]


def join_kernel(z, *refs):
    for flip in range(z.ranks):
        refs[z.ranks][flip] = refs[flip][...]


def project_kernel(z, *refs):
    token_refs = refs[: z.tps]
    weight_refs = refs[z.tps : 2 * z.tps]
    own_ref = refs[2 * z.tps]
    out_refs = refs[2 * z.tps + 1 : 2 * z.tps + z.ranks]
    inputs, total = refs[2 * z.tps + z.ranks :]
    me = lax.axis_index("seq")
    for t in range(z.tps):
        for flip in range(z.ranks):
            source = me ^ flip
            for slot in range(z.whole):
                rows = pl.ds(aligned(slot * z.ranks + source, z.part), z.part)
                lanes = slice(slot * z.tokens, (slot + 1) * z.tokens)
                inputs[t, rows, :] = token_refs[t][flip, :, lanes]
            if z.rest:
                head = z.whole * z.ranks + source // z.sharers
                wide = z.strip * z.block_rows
                at = pl.ds(aligned(source % z.sharers, wide), wide)
                lanes = slice(z.whole * z.tokens, z.whole * z.tokens + wide)
                inputs[t, pl.ds(aligned(head, z.part), z.part), at] = token_refs[t][flip, :, lanes]
    acc = None
    for t in range(z.tps):
        w = weight_refs[t][...].reshape(z.heads * z.part, z.cols)
        term = lax.dot_general(
            inputs[t], w, (((0,), (0,)), ((), ())), preferred_element_type=jnp.float32
        )
        acc = term if acc is None else acc + term
    total[...] = acc.reshape(z.blocks, z.ranks, z.rows, z.cols)
    for b in range(z.blocks):
        own_ref[b] = total[b, me]
        for flip in range(1, z.ranks):
            out_refs[flip - 1][b] = total[b, me ^ flip].astype(jnp.bfloat16)


def local_call(kernel, outs, scratch=(), smem=0, name=None, limit=16):
    def call(*args):
        specs = [
            pl.BlockSpec(memory_space=pltpu.SMEM if i < smem else pltpu.VMEM)
            for i in range(len(args))
        ]
        return pl.pallas_call(
            kernel,
            out_shape=outs,
            in_specs=specs,
            out_specs=[pl.BlockSpec(memory_space=pltpu.VMEM)] * len(outs),
            scratch_shapes=list(scratch),
            compiler_params=pltpu.CompilerParams(vmem_limit_bytes=limit << 20),
            name=name,
        )(*args)

    return call


def stationary_plan(z, queries, key_vectors, value_vectors, block_mask, out_weight):
    bf16 = jnp.bfloat16
    shape = jax.ShapeDtypeStruct
    packed = local_call(
        functools.partial(pack_kernel, z),
        [shape((z.units, z.rows, z.hd), bf16)] * z.ranks,
        name="pack",
    )(queries, key_vectors, value_vectors)
    parts = [packed[0]] + [exchange(packed[f], "seq", f) for f in range(1, z.ranks)]
    sliced = local_call(
        functools.partial(weight_kernel, z),
        [shape((z.heads, z.part, z.cols), bf16)] * z.tps,
        name="weight_slices",
    )(out_weight)
    weights = [sliced[0]] + [exchange(sliced[f], "tp", f) for f in range(1, z.tps)]
    parts, weights = lax.optimization_barrier((parts, weights))
    strips = local_call(
        functools.partial(attend_kernel, z),
        [shape((z.part, z.out_tokens), bf16)] * z.ranks,
        scratch=[
            pltpu.VMEM((z.slots, z.tokens, z.hd), bf16),
            pltpu.VMEM((z.slots, z.tokens, z.hd), bf16),
            pltpu.VMEM((z.slots, z.tokens, z.hd), bf16),
            pltpu.VMEM((z.tokens, z.tokens), bf16),
            pltpu.VMEM((z.hd, z.out_tokens), bf16),
        ],
        smem=1,
        name="attend",
    )(block_mask, *parts)
    strips = [strips[0]] + [exchange(strips[f], "seq", f) for f in range(1, z.ranks)]
    joined = local_call(
        functools.partial(join_kernel, z),
        [shape((z.ranks, z.part, z.out_tokens), bf16)],
        name="join",
    )(*strips)[0]
    tokens = [joined]
    flip = z.tps // 2
    tokens = {0: joined}
    while flip:
        for held in list(tokens):
            tokens[held ^ flip] = exchange(tokens[held], "tp", flip)
        flip //= 2
    sums = local_call(
        functools.partial(project_kernel, z),
        [shape((z.blocks, z.rows, z.cols), jnp.float32)]
        + [shape((z.blocks, z.rows, z.cols), bf16)] * (z.ranks - 1),
        scratch=[
            pltpu.VMEM((z.tps, z.heads * z.part, z.tokens), bf16),
            pltpu.VMEM((z.blocks, z.ranks, z.rows, z.cols), jnp.float32),
        ],
        name="project",
    )(*[tokens[t] for t in range(z.tps)], *weights)
    total = sums[0]
    for f in range(1, z.ranks):
        total = total + exchange(sums[f], "seq", f).astype(jnp.float32)
    return total.astype(bf16)


def body(queries, key_vectors, value_vectors, block_mask, out_weight):
    z = Sizes(
        lax.axis_size("seq"),
        lax.axis_size("tp"),
        queries.shape,
        block_mask.shape[0],
        out_weight.shape,
    )
    plan = functools.partial(stationary_plan, z) if z.fits() else gathered_plan
    return plan(queries, key_vectors, value_vectors, block_mask, out_weight)


def solution(mesh):
    return jax.shard_map(
        body,
        mesh=mesh,
        in_specs=(
            P("groups", "seq", "tp"),
            P("groups", "seq", "tp"),
            P("groups", "seq", "tp"),
            P("tp", None, None),
            P("tp", "seq", None),
        ),
        out_specs=P("groups", "seq", "tp"),
        check_vma=False,
    )
```

```python
import functools

import jax
import jax.numpy as jnp
import numpy as np
from jax import lax
from jax.experimental import pallas as pl
from jax.experimental.pallas import tpu as pltpu
from jax.sharding import PartitionSpec as P


KEYS = 28


def strip_tables(heads_local, blocks, slot_total):
    slot_ids = np.arange(slot_total)
    head_of = slot_ids * heads_local // slot_total
    per_head = np.bincount(head_of, minlength=heads_local)
    head_begin = np.cumsum(per_head) - per_head
    order_in_head = slot_ids - head_begin[head_of]
    head_share = per_head[head_of]
    first_block = order_in_head * blocks // head_share
    block_count = (order_in_head + 1) * blocks // head_share - first_block
    return (head_of, first_block, block_count)


def gathered_plan(queries, key_vectors, value_vectors, block_mask, out_weight):
    rank_count = lax.axis_size("seq")
    my_rank = lax.axis_index("seq")
    block_total, row_share, feature_width = queries.shape
    heads_local = block_mask.shape[0]
    head_size = feature_width // heads_local
    block_rows = row_share * rank_count
    per_rank = (heads_local + rank_count - 1) // rank_count
    slot_total = rank_count * per_rank
    least_share = slot_total // heads_local
    strip_cap = ((block_total + least_share - 1) // least_share + 1) // 2 * 2
    key_cap = min(KEYS, block_total)
    head_of, first_block, block_count = strip_tables(heads_local, block_total, slot_total)
    slot_grid = np.arange(slot_total).reshape(rank_count, per_rank).T
    paired = jnp.concatenate(
        [
            key_vectors.reshape(block_total, row_share, heads_local, head_size),
            value_vectors.reshape(block_total, row_share, heads_local, head_size),
        ],
        axis=3,
    )
    send_heads = jnp.asarray(head_of[slot_grid].reshape(-1), jnp.int32)
    chosen = jnp.take(paired, send_heads, axis=2)
    chosen = chosen.reshape(block_total, row_share, per_rank, rank_count, 2 * head_size)
    outgoing_pairs = chosen.transpose(2, 0, 3, 1, 4).reshape(
        per_rank, block_total, block_rows, 2 * head_size
    )
    flat_queries = queries.reshape(block_total, row_share, heads_local, head_size).transpose(
        0, 2, 1, 3
    )
    flat_queries = flat_queries.reshape(block_total * heads_local, row_share, head_size)
    positions = np.arange(strip_cap)
    unit_block = first_block[slot_grid][:, None, :] + positions[None, :, None]
    is_live = positions[None, :, None] < block_count[slot_grid][:, None, :]
    unit_index = np.where(is_live, unit_block * heads_local + head_of[slot_grid][:, None, :], 0)
    picked = jnp.take(flat_queries, jnp.asarray(unit_index.reshape(-1), jnp.int32), axis=0)
    picked = jnp.where(
        jnp.asarray(is_live.reshape(-1))[:, None, None], picked, jnp.zeros_like(picked)
    )
    outgoing_queries = picked.reshape(per_rank, strip_cap, block_rows, head_size)
    strip_queries, strip_pairs = (
        lax.all_to_all(outgoing_queries, "seq", split_axis=2, concat_axis=2, tiled=True),
        lax.all_to_all(outgoing_pairs, "seq", split_axis=2, concat_axis=2, tiled=True),
    )
    my_slots = my_rank * per_rank + jnp.arange(per_rank, dtype=jnp.int32)
    my_heads = jnp.asarray(head_of, jnp.int32)[my_slots]
    my_first = jnp.asarray(first_block, jnp.int32)[my_slots]
    query_blocks = jnp.minimum(
        my_first[:, None] + jnp.arange(strip_cap, dtype=jnp.int32)[None, :], block_total - 1
    )
    mask_rows = block_mask[my_heads[:, None], query_blocks]
    column_ids = jnp.arange(block_total, dtype=jnp.int32)
    ranking = (1 - mask_rows) * block_total + column_ids
    key_pick = jnp.argsort(ranking, axis=-1)[..., :key_cap]
    key_live = jnp.take_along_axis(mask_rows, key_pick, axis=-1)
    group_total = per_rank * strip_cap // 2
    query_groups = strip_queries.reshape(group_total, 2, block_rows, head_size)
    pick_groups = key_pick.reshape(group_total, 2, key_cap)
    live_groups = key_live.reshape(group_total, 2, key_cap)
    slot_of_group = jnp.arange(group_total, dtype=jnp.int32) // (strip_cap // 2)
    score_scale = head_size ** (-0.5)

    def attend_group(inputs):
        query_tile, pick_tile, live_tile, slot_index = inputs
        pairs_here = strip_pairs[slot_index]
        gathered = pairs_here[pick_tile]
        scores = (
            jnp.einsum(
                "qid,qkjd->qikj",
                query_tile,
                gathered[..., :head_size],
                preferred_element_type=jnp.float32,
            )
            * score_scale
        )
        allowed = (live_tile > 0)[:, None, :, None]
        scores = jnp.where(allowed, scores, -jnp.inf)
        largest = jnp.max(scores, axis=(2, 3), keepdims=True)
        weights = jnp.exp(scores - largest)
        totals = jnp.sum(weights, axis=(2, 3))
        blended = jnp.einsum(
            "qikj,qkjd->qid",
            weights.astype(jnp.bfloat16),
            gathered[..., head_size:],
            preferred_element_type=jnp.float32,
        )
        return (blended / totals[..., None]).astype(jnp.bfloat16)

    strip_out = lax.map(attend_group, (query_groups, pick_groups, live_groups, slot_of_group))
    outgoing_out = strip_out.reshape(per_rank, strip_cap, block_rows, head_size)
    returned = lax.all_to_all(outgoing_out, "seq", split_axis=2, concat_axis=2, tiled=True)
    slot_mesh, step_mesh = np.meshgrid(np.arange(slot_total), positions, indexing="ij")
    live_slot = step_mesh < block_count[slot_mesh]
    placement_index = np.zeros((block_total, heads_local), np.int64)
    source_index = (
        slot_mesh % per_rank * strip_cap + step_mesh
    ) * rank_count + slot_mesh // per_rank
    placement_index[
        first_block[slot_mesh][live_slot] + step_mesh[live_slot], head_of[slot_mesh][live_slot]
    ] = source_index[live_slot]
    flat_back = returned.reshape(per_rank * strip_cap * rank_count, row_share, head_size)
    own_out = jnp.take(flat_back, jnp.asarray(placement_index.reshape(-1), jnp.int32), axis=0)
    own_out = own_out.reshape(block_total, heads_local, row_share, head_size)
    token_total = block_total * row_share
    token_out = own_out.transpose(0, 2, 1, 3).reshape(token_total, heads_local, head_size)
    partial_sum = jnp.einsum(
        "thd,hdo->to",
        token_out,
        lax.all_gather(out_weight, "seq", axis=1, tiled=True),
        preferred_element_type=jnp.float32,
    )
    summed = lax.psum_scatter(
        partial_sum.astype(jnp.bfloat16), "tp", scatter_dimension=1, tiled=True
    ).astype(jnp.float32)
    return summed.astype(jnp.bfloat16).reshape(block_total, row_share, summed.shape[1])


def exchange(array, axis, flip):
    size = lax.axis_size(axis)
    return lax.ppermute(array, axis, [(i, i ^ flip) for i in range(size)])


def aligned(index, unit):
    return pl.multiple_of(index * unit, unit)


class Sizes:
    def __init__(self, rank_count, tp_count, queries_shape, heads_local, weight_shape):
        self.ranks = rank_count
        self.tps = tp_count
        self.blocks, self.rows, width = queries_shape
        self.heads = heads_local
        self.hd = width // heads_local
        self.whole = heads_local // rank_count
        self.rest = heads_local % rank_count
        self.sharers = rank_count // self.rest if self.rest else 1
        self.strip = self.blocks // self.sharers if self.rest else 0
        self.slots = self.whole + (1 if self.rest else 0)
        self.q_units = self.whole * self.blocks + self.strip
        self.kv_units = self.slots * self.blocks
        self.units = self.q_units + 2 * self.kv_units
        self.block_rows = self.rows * rank_count
        self.tokens = self.blocks * self.block_rows
        self.out_tokens = self.q_units * self.block_rows
        self.part = weight_shape[1]
        self.dout = weight_shape[2]
        self.cols = self.dout // tp_count

    def fits(self):
        power = lambda n: n & (n - 1) == 0
        if not (power(self.ranks) and power(self.tps) and self.whole > 0):
            return False
        if self.rest and (self.ranks % self.rest or self.blocks % self.sharers):
            return False
        if self.rows % 32 or self.part % 32 or self.hd % 128 or self.cols % 128:
            return False
        gathered = (self.ranks - 1) * self.heads * self.part * self.dout
        summed = (self.ranks - 1) * self.tokens // self.ranks * self.cols
        summed += (self.tps - 1) * self.heads * self.part * (self.cols + self.tokens)
        return summed < gathered


def pack_kernel(z, q_hbm, k_hbm, v_hbm, *refs):
    out_refs = refs[: z.ranks]
    q_ref, k_ref, v_ref, sems = refs[z.ranks :]
    me = lax.axis_index("seq")
    copies = [
        pltpu.make_async_copy(source, target, sems.at[i])
        for i, (source, target) in enumerate(
            ((q_hbm, q_ref), (k_hbm, k_ref), (v_hbm, v_ref))
        )
    ]
    for copy in copies:
        copy.start()
    for copy, ref, begin, strip in (
        (copies[0], q_ref, 0, z.strip),
        (copies[1], k_ref, z.q_units, z.blocks),
        (copies[2], v_ref, z.q_units + z.kv_units, z.blocks),
    ):
        copy.wait()
        for flip in range(z.ranks):
            peer = me ^ flip
            for slot in range(z.whole):
                cols = pl.ds(aligned(slot * z.ranks + peer, z.hd), z.hd)
                at = begin + slot * z.blocks
                out_refs[flip][at : at + z.blocks] = ref[:, :, cols]
            if z.rest:
                cols = pl.ds(aligned(z.whole * z.ranks + peer // z.sharers, z.hd), z.hd)
                first = (peer % z.sharers) * z.strip if strip < z.blocks else 0
                at = begin + z.whole * z.blocks
                out_refs[flip][at : at + strip] = ref[pl.ds(first, strip), :, cols]


def weight_kernel(z, w_hbm, *refs):
    out_refs, sems = refs[: z.tps], refs[z.tps]
    me = lax.axis_index("tp")
    copies = [
        pltpu.make_async_copy(
            w_hbm.at[:, :, pl.ds(aligned(me ^ flip, z.cols), z.cols)],
            out_refs[flip],
            sems.at[flip],
        )
        for flip in range(z.tps)
    ]
    for copy in copies:
        copy.start()
    for copy in copies:
        copy.wait()


def attend_kernel(z, mask_ref, *refs):
    part_refs = refs[: z.ranks]
    out_refs = refs[z.ranks : 2 * z.ranks]
    query, keys, values, weights, result = refs[2 * z.ranks :]
    me = lax.axis_index("seq")
    scale = z.hd ** (-0.5)
    for slot in range(z.slots):
        is_strip = slot >= z.whole
        count = z.strip if is_strip else z.blocks
        head = z.whole * z.ranks + me // z.sharers if is_strip else slot * z.ranks + me
        first = (me % z.sharers) * z.strip if is_strip else 0
        for flip in range(z.ranks):
            source = me ^ flip
            for b in range(count):
                rows = pl.ds(b * z.block_rows + aligned(source, z.rows), z.rows)
                query[slot, rows, :] = part_refs[flip][slot * z.blocks + b]
            for b in range(z.blocks):
                rows = pl.ds(b * z.block_rows + flip * z.rows, z.rows)
                unit = z.q_units + slot * z.blocks + b
                keys[slot, rows, :] = part_refs[flip][unit]
                values[slot, rows, :] = part_refs[flip][unit + z.kv_units]
        wide = count * z.block_rows
        inverses = []
        for b in range(count):
            lanes = slice(b * z.block_rows, (b + 1) * z.block_rows)
            scores = (
                lax.dot_general(
                    keys[slot],
                    query[slot, lanes, :],
                    (((1,), (1,)), ((), ())),
                    preferred_element_type=jnp.float32,
                )
                * scale
            )
            tiles = []
            for t in range(z.blocks):
                tile = scores[t * z.block_rows : (t + 1) * z.block_rows]
                tiles.append(jnp.where(mask_ref[head, first + b, t] > 0, tile, -jnp.inf))
            scores = jnp.concatenate(tiles, axis=0)
            largest = jnp.max(scores, axis=0, keepdims=True)
            exps = jnp.exp(scores - largest)
            inverses.append(jnp.sum(exps, axis=0, keepdims=True))
            weights[:, lanes] = exps.astype(jnp.bfloat16)
        blended = lax.dot_general(
            values[slot],
            weights[:, :wide],
            (((0,), (0,)), ((), ())),
            preferred_element_type=jnp.float32,
        )
        blended = blended / jnp.concatenate(inverses, axis=1)
        lanes = slice(slot * z.tokens, slot * z.tokens + wide)
        result[:, lanes] = blended.astype(jnp.bfloat16)
    for flip in range(z.ranks):
        out_refs[flip][...] = result[pl.ds(aligned(me ^ flip, z.part), z.part), :]


def join_kernel(z, *refs):
    for flip in range(z.ranks):
        refs[z.ranks][flip] = refs[flip][...]


def project_kernel(z, *refs):
    token_refs = refs[: z.tps]
    weight_refs = refs[z.tps : 2 * z.tps]
    own_ref = refs[2 * z.tps]
    out_refs = refs[2 * z.tps + 1 : 2 * z.tps + z.ranks]
    inputs, total = refs[2 * z.tps + z.ranks :]
    me = lax.axis_index("seq")
    for t in range(z.tps):
        for flip in range(z.ranks):
            source = me ^ flip
            for slot in range(z.whole):
                rows = pl.ds(aligned(slot * z.ranks + source, z.part), z.part)
                lanes = slice(slot * z.tokens, (slot + 1) * z.tokens)
                inputs[t, rows, :] = token_refs[t][flip, :, lanes]
            if z.rest:
                head = z.whole * z.ranks + source // z.sharers
                wide = z.strip * z.block_rows
                at = pl.ds(aligned(source % z.sharers, wide), wide)
                lanes = slice(z.whole * z.tokens, z.whole * z.tokens + wide)
                inputs[t, pl.ds(aligned(head, z.part), z.part), at] = token_refs[t][flip, :, lanes]
    acc = None
    for t in range(z.tps):
        w = weight_refs[t][...].reshape(z.heads * z.part, z.cols)
        term = lax.dot_general(
            inputs[t], w, (((0,), (0,)), ((), ())), preferred_element_type=jnp.float32
        )
        acc = term if acc is None else acc + term
    total[...] = acc.reshape(z.blocks, z.ranks, z.rows, z.cols)
    for b in range(z.blocks):
        own_ref[b] = total[b, me]
        for flip in range(1, z.ranks):
            out_refs[flip - 1][b] = total[b, me ^ flip].astype(jnp.bfloat16)


def local_call(kernel, outs, scratch=(), places=None, limit=16):
    def call(*args):
        spaces = places or [pltpu.VMEM] * len(args)
        args = [
            pltpu.with_memory_space_constraint(arg, space) if space is pltpu.HBM else arg
            for arg, space in zip(args, spaces)
        ]
        return pl.pallas_call(
            kernel,
            out_shape=outs,
            in_specs=[pl.BlockSpec(memory_space=space) for space in spaces],
            out_specs=[pl.BlockSpec(memory_space=pltpu.VMEM)] * len(outs),
            scratch_shapes=list(scratch),
            compiler_params=pltpu.CompilerParams(vmem_limit_bytes=limit << 20),
        )(*args)

    return call


def exchange_all(arrays, axis):
    got = [arrays[0]]
    for flip in range(1, len(arrays)):
        got.append(exchange(arrays[flip], axis, flip))
    return got


def stationary_plan(z, queries, key_vectors, value_vectors, block_mask, out_weight):
    bf16 = jnp.bfloat16
    shape = jax.ShapeDtypeStruct
    held = pltpu.VMEM(queries.shape, bf16)
    packed = local_call(
        functools.partial(pack_kernel, z),
        [shape((z.units, z.rows, z.hd), bf16)] * z.ranks,
        scratch=[held, held, held, pltpu.SemaphoreType.DMA((3,))],
        places=[pltpu.HBM] * 3,
    )(queries, key_vectors, value_vectors)
    parts = exchange_all(packed, "seq")
    sliced = local_call(
        functools.partial(weight_kernel, z),
        [shape((z.heads, z.part, z.cols), bf16)] * z.tps,
        scratch=[pltpu.SemaphoreType.DMA((z.tps,))],
        places=[pltpu.HBM],
    )(out_weight)
    weights = exchange_all(sliced, "tp")
    parts, weights = lax.optimization_barrier((parts, weights))
    slot_rows = pltpu.VMEM((z.slots, z.tokens, z.hd), bf16)
    strips = local_call(
        functools.partial(attend_kernel, z),
        [shape((z.part, z.out_tokens), bf16)] * z.ranks,
        scratch=[slot_rows, slot_rows, slot_rows]
        + [pltpu.VMEM((z.tokens, z.tokens), bf16), pltpu.VMEM((z.hd, z.out_tokens), bf16)],
        places=[pltpu.SMEM] + [pltpu.VMEM] * z.ranks,
    )(block_mask, *parts)
    pieces = exchange_all(strips, "seq")

    def join(arrays):
        return local_call(
            functools.partial(join_kernel, z), [shape((z.ranks, z.part, z.out_tokens), bf16)]
        )(*arrays)[0]

    tokens = {0: join(pieces)}
    flip = z.tps // 2
    if flip:
        far = []
        for piece in pieces:
            far.append(exchange(piece, "tp", flip))
        tokens[flip] = join(far)
        flip //= 2
    while flip:
        for has in list(tokens):
            tokens[has ^ flip] = exchange(tokens[has], "tp", flip)
        flip //= 2
    sums = local_call(
        functools.partial(project_kernel, z),
        [shape((z.blocks, z.rows, z.cols), jnp.float32)]
        + [shape((z.blocks, z.rows, z.cols), bf16)] * (z.ranks - 1),
        scratch=[
            pltpu.VMEM((z.tps, z.heads * z.part, z.tokens), bf16),
            pltpu.VMEM((z.blocks, z.ranks, z.rows, z.cols), jnp.float32),
        ],
    )(*[tokens[t] for t in range(z.tps)], *weights)
    got = exchange_all(sums, "seq")
    total = got[0]
    for term in got[1:]:
        total = total + term.astype(jnp.float32)
    return total.astype(bf16)


def body(queries, key_vectors, value_vectors, block_mask, out_weight):
    z = Sizes(
        lax.axis_size("seq"),
        lax.axis_size("tp"),
        queries.shape,
        block_mask.shape[0],
        out_weight.shape,
    )
    if not z.fits():
        return gathered_plan(queries, key_vectors, value_vectors, block_mask, out_weight)
    return stationary_plan(z, queries, key_vectors, value_vectors, block_mask, out_weight)


def solution(mesh):
    return jax.shard_map(
        body,
        mesh=mesh,
        in_specs=(
            P("groups", "seq", "tp"),
            P("groups", "seq", "tp"),
            P("groups", "seq", "tp"),
            P("tp", None, None),
            P("tp", "seq", None),
        ),
        out_specs=P("groups", "seq", "tp"),
        check_vma=False,
    )
```

```python
import functools

import jax
import jax.numpy as jnp
import numpy as np
from jax import lax
from jax.experimental import pallas as pl
from jax.experimental.pallas import tpu as pltpu
from jax.sharding import PartitionSpec as P


KEYS = 28


def strip_tables(heads_local, blocks, slot_total):
    slot_ids = np.arange(slot_total)
    head_of = slot_ids * heads_local // slot_total
    per_head = np.bincount(head_of, minlength=heads_local)
    head_begin = np.cumsum(per_head) - per_head
    order_in_head = slot_ids - head_begin[head_of]
    head_share = per_head[head_of]
    first_block = order_in_head * blocks // head_share
    block_count = (order_in_head + 1) * blocks // head_share - first_block
    return (head_of, first_block, block_count)


def gathered_plan(queries, key_vectors, value_vectors, block_mask, out_weight):
    rank_count = lax.axis_size("seq")
    my_rank = lax.axis_index("seq")
    block_total, row_share, feature_width = queries.shape
    heads_local = block_mask.shape[0]
    head_size = feature_width // heads_local
    block_rows = row_share * rank_count
    per_rank = (heads_local + rank_count - 1) // rank_count
    slot_total = rank_count * per_rank
    least_share = slot_total // heads_local
    strip_cap = ((block_total + least_share - 1) // least_share + 1) // 2 * 2
    key_cap = min(KEYS, block_total)
    head_of, first_block, block_count = strip_tables(heads_local, block_total, slot_total)
    slot_grid = np.arange(slot_total).reshape(rank_count, per_rank).T
    paired = jnp.concatenate(
        [
            key_vectors.reshape(block_total, row_share, heads_local, head_size),
            value_vectors.reshape(block_total, row_share, heads_local, head_size),
        ],
        axis=3,
    )
    send_heads = jnp.asarray(head_of[slot_grid].reshape(-1), jnp.int32)
    chosen = jnp.take(paired, send_heads, axis=2)
    chosen = chosen.reshape(block_total, row_share, per_rank, rank_count, 2 * head_size)
    outgoing_pairs = chosen.transpose(2, 0, 3, 1, 4).reshape(
        per_rank, block_total, block_rows, 2 * head_size
    )
    flat_queries = queries.reshape(block_total, row_share, heads_local, head_size).transpose(
        0, 2, 1, 3
    )
    flat_queries = flat_queries.reshape(block_total * heads_local, row_share, head_size)
    positions = np.arange(strip_cap)
    unit_block = first_block[slot_grid][:, None, :] + positions[None, :, None]
    is_live = positions[None, :, None] < block_count[slot_grid][:, None, :]
    unit_index = np.where(is_live, unit_block * heads_local + head_of[slot_grid][:, None, :], 0)
    picked = jnp.take(flat_queries, jnp.asarray(unit_index.reshape(-1), jnp.int32), axis=0)
    picked = jnp.where(
        jnp.asarray(is_live.reshape(-1))[:, None, None], picked, jnp.zeros_like(picked)
    )
    outgoing_queries = picked.reshape(per_rank, strip_cap, block_rows, head_size)
    strip_queries, strip_pairs = (
        lax.all_to_all(outgoing_queries, "seq", split_axis=2, concat_axis=2, tiled=True),
        lax.all_to_all(outgoing_pairs, "seq", split_axis=2, concat_axis=2, tiled=True),
    )
    my_slots = my_rank * per_rank + jnp.arange(per_rank, dtype=jnp.int32)
    my_heads = jnp.asarray(head_of, jnp.int32)[my_slots]
    my_first = jnp.asarray(first_block, jnp.int32)[my_slots]
    query_blocks = jnp.minimum(
        my_first[:, None] + jnp.arange(strip_cap, dtype=jnp.int32)[None, :], block_total - 1
    )
    mask_rows = block_mask[my_heads[:, None], query_blocks]
    column_ids = jnp.arange(block_total, dtype=jnp.int32)
    ranking = (1 - mask_rows) * block_total + column_ids
    key_pick = jnp.argsort(ranking, axis=-1)[..., :key_cap]
    key_live = jnp.take_along_axis(mask_rows, key_pick, axis=-1)
    group_total = per_rank * strip_cap // 2
    query_groups = strip_queries.reshape(group_total, 2, block_rows, head_size)
    pick_groups = key_pick.reshape(group_total, 2, key_cap)
    live_groups = key_live.reshape(group_total, 2, key_cap)
    slot_of_group = jnp.arange(group_total, dtype=jnp.int32) // (strip_cap // 2)
    score_scale = head_size ** (-0.5)

    def attend_group(inputs):
        query_tile, pick_tile, live_tile, slot_index = inputs
        pairs_here = strip_pairs[slot_index]
        gathered = pairs_here[pick_tile]
        scores = (
            jnp.einsum(
                "qid,qkjd->qikj",
                query_tile,
                gathered[..., :head_size],
                preferred_element_type=jnp.float32,
            )
            * score_scale
        )
        allowed = (live_tile > 0)[:, None, :, None]
        scores = jnp.where(allowed, scores, -jnp.inf)
        largest = jnp.max(scores, axis=(2, 3), keepdims=True)
        weights = jnp.exp(scores - largest)
        totals = jnp.sum(weights, axis=(2, 3))
        blended = jnp.einsum(
            "qikj,qkjd->qid",
            weights.astype(jnp.bfloat16),
            gathered[..., head_size:],
            preferred_element_type=jnp.float32,
        )
        return (blended / totals[..., None]).astype(jnp.bfloat16)

    strip_out = lax.map(attend_group, (query_groups, pick_groups, live_groups, slot_of_group))
    outgoing_out = strip_out.reshape(per_rank, strip_cap, block_rows, head_size)
    returned = lax.all_to_all(outgoing_out, "seq", split_axis=2, concat_axis=2, tiled=True)
    slot_mesh, step_mesh = np.meshgrid(np.arange(slot_total), positions, indexing="ij")
    live_slot = step_mesh < block_count[slot_mesh]
    placement_index = np.zeros((block_total, heads_local), np.int64)
    source_index = (
        slot_mesh % per_rank * strip_cap + step_mesh
    ) * rank_count + slot_mesh // per_rank
    placement_index[
        first_block[slot_mesh][live_slot] + step_mesh[live_slot], head_of[slot_mesh][live_slot]
    ] = source_index[live_slot]
    flat_back = returned.reshape(per_rank * strip_cap * rank_count, row_share, head_size)
    own_out = jnp.take(flat_back, jnp.asarray(placement_index.reshape(-1), jnp.int32), axis=0)
    own_out = own_out.reshape(block_total, heads_local, row_share, head_size)
    token_total = block_total * row_share
    token_out = own_out.transpose(0, 2, 1, 3).reshape(token_total, heads_local, head_size)
    partial_sum = jnp.einsum(
        "thd,hdo->to",
        token_out,
        lax.all_gather(out_weight, "seq", axis=1, tiled=True),
        preferred_element_type=jnp.float32,
    )
    summed = lax.psum_scatter(
        partial_sum.astype(jnp.bfloat16), "tp", scatter_dimension=1, tiled=True
    ).astype(jnp.float32)
    return summed.astype(jnp.bfloat16).reshape(block_total, row_share, summed.shape[1])


def exchange(array, axis, flip):
    size = lax.axis_size(axis)
    return lax.ppermute(array, axis, [(i, i ^ flip) for i in range(size)])


def aligned(index, unit):
    return pl.multiple_of(index * unit, unit)


class Sizes:
    def __init__(self, rank_count, tp_count, queries_shape, heads_local, weight_shape):
        self.ranks = rank_count
        self.tps = tp_count
        self.blocks, self.rows, width = queries_shape
        self.heads = heads_local
        self.hd = width // heads_local
        self.whole = heads_local // rank_count
        self.rest = heads_local % rank_count
        self.sharers = rank_count // self.rest if self.rest else 1
        self.strip = self.blocks // self.sharers if self.rest else 0
        self.slots = self.whole + (1 if self.rest else 0)
        self.q_units = self.whole * self.blocks + self.strip
        self.kv_units = self.slots * self.blocks
        self.units = self.q_units + 2 * self.kv_units
        self.block_rows = self.rows * rank_count
        self.tokens = self.blocks * self.block_rows
        self.out_tokens = self.q_units * self.block_rows
        self.part = weight_shape[1]
        self.dout = weight_shape[2]
        self.cols = self.dout // tp_count

    def fits(self):
        power = lambda n: n & (n - 1) == 0
        if not (power(self.ranks) and power(self.tps) and self.whole > 0):
            return False
        if self.rest and (self.ranks % self.rest or self.blocks % self.sharers):
            return False
        if self.rows % 32 or self.part % 32 or self.hd % 128 or self.cols % 128:
            return False
        gathered = (self.ranks - 1) * self.heads * self.part * self.dout
        summed = (self.ranks - 1) * self.tokens // self.ranks * self.cols
        summed += (self.tps - 1) * self.heads * self.part * (self.cols + self.tokens)
        return summed < gathered


def run_copies(pairs, sems):
    copies = [pltpu.make_async_copy(a, b, sems.at[i]) for i, (a, b) in enumerate(pairs)]
    for copy in copies:
        copy.start()
    for copy in copies:
        copy.wait()


def pack_kernel(z, q_hbm, k_hbm, v_hbm, *refs):
    out_refs = refs[: z.ranks]
    q_ref, k_ref, v_ref, sems = refs[z.ranks :]
    me = lax.axis_index("seq")
    arrays = ((q_hbm, q_ref, 0), (k_hbm, k_ref, z.q_units), (v_hbm, v_ref, z.q_units + z.kv_units))
    copies = []
    for i, (hbm, ref, _) in enumerate(arrays):
        for b in range(z.blocks):
            copies.append(pltpu.make_async_copy(hbm.at[b], ref.at[b], sems.at[i * z.blocks + b]))
    for copy in copies:
        copy.start()
    for i, (_, ref, begin) in enumerate(arrays):
        for b in range(z.blocks):
            copies[i * z.blocks + b].wait()
            for flip in range(z.ranks):
                for slot in range(z.whole):
                    cols = pl.ds(aligned(slot * z.ranks + (me ^ flip), z.hd), z.hd)
                    out_refs[flip][begin + slot * z.blocks + b] = ref[b, :, cols]
        if z.rest:
            count = z.strip if i == 0 else z.blocks
            for flip in range(z.ranks):
                peer = me ^ flip
                cols = pl.ds(aligned(z.whole * z.ranks + peer // z.sharers, z.hd), z.hd)
                first = (peer % z.sharers) * z.strip if i == 0 else 0
                at = begin + z.whole * z.blocks
                out_refs[flip][at : at + count] = ref[pl.ds(first, count), :, cols]


def weight_kernel(z, w_hbm, *refs):
    out_refs, sems = refs[: z.tps], refs[z.tps]
    me = lax.axis_index("tp")
    pairs = []
    for head in range(z.heads):
        for flip in range(z.tps):
            cols = pl.ds(aligned(me ^ flip, z.cols), z.cols)
            pairs.append((w_hbm.at[head, :, cols], out_refs[flip].at[head]))
    run_copies(pairs, sems)


def attend_kernel(z, mask_ref, *refs):
    part_refs = refs[: z.ranks]
    out_refs = refs[z.ranks : 2 * z.ranks]
    query, keys, values, weights, result = refs[2 * z.ranks :]
    me = lax.axis_index("seq")
    scale = z.hd ** (-0.5)
    for slot in range(z.slots):
        is_strip = slot >= z.whole
        count = z.strip if is_strip else z.blocks
        head = z.whole * z.ranks + me // z.sharers if is_strip else slot * z.ranks + me
        first = (me % z.sharers) * z.strip if is_strip else 0
        for flip in range(z.ranks):
            source = me ^ flip
            for b in range(count):
                rows = pl.ds(b * z.block_rows + aligned(source, z.rows), z.rows)
                query[slot, rows, :] = part_refs[flip][slot * z.blocks + b]
            for b in range(z.blocks):
                rows = pl.ds(b * z.block_rows + flip * z.rows, z.rows)
                unit = z.q_units + slot * z.blocks + b
                keys[slot, rows, :] = part_refs[flip][unit]
                values[slot, rows, :] = part_refs[flip][unit + z.kv_units]
        wide = count * z.block_rows
        inverses = []
        for b in range(count):
            lanes = slice(b * z.block_rows, (b + 1) * z.block_rows)
            scores = (
                lax.dot_general(
                    keys[slot],
                    query[slot, lanes, :],
                    (((1,), (1,)), ((), ())),
                    preferred_element_type=jnp.float32,
                )
                * scale
            )
            tiles = []
            for t in range(z.blocks):
                tile = scores[t * z.block_rows : (t + 1) * z.block_rows]
                tiles.append(jnp.where(mask_ref[first + b, t, head] > 0, tile, -jnp.inf))
            scores = jnp.concatenate(tiles, axis=0)
            largest = jnp.max(scores, axis=0, keepdims=True)
            exps = jnp.exp(scores - largest)
            inverses.append(jnp.sum(exps, axis=0, keepdims=True))
            weights[:, lanes] = exps.astype(jnp.bfloat16)
        blended = lax.dot_general(
            values[slot],
            weights[:, :wide],
            (((0,), (0,)), ((), ())),
            preferred_element_type=jnp.float32,
        )
        blended = blended / jnp.concatenate(inverses, axis=1)
        lanes = slice(slot * z.tokens, slot * z.tokens + wide)
        result[:, lanes] = blended.astype(jnp.bfloat16)
    for flip in range(z.ranks):
        out_refs[flip][...] = result[pl.ds(aligned(me ^ flip, z.part), z.part), :]


def join_kernel(z, *refs):
    for flip in range(z.ranks):
        refs[z.ranks][flip] = refs[flip][...]


def project_kernel(z, count, has_total, is_last, *refs):
    token_refs, refs = refs[:count], refs[count:]
    weight_refs, refs = refs[:count], refs[count:]
    if has_total:
        before, refs = refs[0], refs[1:]
    out_refs, inputs = refs[: z.ranks if is_last else 1], refs[z.ranks if is_last else 1]
    me = lax.axis_index("seq")
    acc = before[...].reshape(z.tokens, z.cols) if has_total else None
    for t in range(count):
        for flip in range(z.ranks):
            source = me ^ flip
            for slot in range(z.whole):
                rows = pl.ds(aligned(slot * z.ranks + source, z.part), z.part)
                lanes = slice(slot * z.tokens, (slot + 1) * z.tokens)
                inputs[t, rows, :] = token_refs[t][flip, :, lanes]
            if z.rest:
                head = z.whole * z.ranks + source // z.sharers
                wide = z.strip * z.block_rows
                at = pl.ds(aligned(source % z.sharers, wide), wide)
                lanes = slice(z.whole * z.tokens, z.whole * z.tokens + wide)
                inputs[t, pl.ds(aligned(head, z.part), z.part), at] = token_refs[t][flip, :, lanes]
    for t in range(count):
        w = weight_refs[t][...].reshape(z.heads * z.part, z.cols)
        term = lax.dot_general(
            inputs[t], w, (((0,), (0,)), ((), ())), preferred_element_type=jnp.float32
        )
        acc = term if acc is None else acc + term
    acc = acc.reshape(z.blocks, z.ranks, z.rows, z.cols)
    if not is_last:
        out_refs[0][...] = acc
        return
    total = refs[z.ranks + 1]
    total[...] = acc
    for b in range(z.blocks):
        out_refs[0][b] = total[b, me]
        for flip in range(1, z.ranks):
            out_refs[flip][b] = total[b, me ^ flip].astype(jnp.bfloat16)


def local_call(kernel, outs, scratch=(), places=None, limit=16, flops=1 << 20):
    def call(*args):
        spaces = places or [pltpu.VMEM] * len(args)
        args = [
            pltpu.with_memory_space_constraint(arg, space) if space is pltpu.HBM else arg
            for arg, space in zip(args, spaces)
        ]
        return pl.pallas_call(
            kernel,
            out_shape=outs,
            in_specs=[pl.BlockSpec(memory_space=space) for space in spaces],
            out_specs=[pl.BlockSpec(memory_space=pltpu.VMEM)] * len(outs),
            scratch_shapes=list(scratch),
            compiler_params=pltpu.CompilerParams(vmem_limit_bytes=limit << 20),
            cost_estimate=pl.CostEstimate(flops=flops, bytes_accessed=1 << 20, transcendentals=0),
        )(*args)

    return call


def exchange_all(arrays, axis):
    got = [arrays[0]]
    for flip in range(1, len(arrays)):
        got.append(exchange(arrays[flip], axis, flip))
    return got


def stationary_plan(z, queries, key_vectors, value_vectors, block_mask, out_weight):
    bf16 = jnp.bfloat16
    shape = jax.ShapeDtypeStruct
    packed = local_call(
        functools.partial(pack_kernel, z),
        [shape((z.units, z.rows, z.hd), bf16)] * z.ranks,
        scratch=[pltpu.VMEM(queries.shape, bf16)] * 3
        + [pltpu.SemaphoreType.DMA((3 * z.blocks,))],
        places=[pltpu.HBM] * 3,
    )(queries, key_vectors, value_vectors)
    parts = exchange_all(packed, "seq")
    sliced = local_call(
        functools.partial(weight_kernel, z),
        [shape((z.heads, z.part, z.cols), bf16)] * z.tps,
        scratch=[pltpu.SemaphoreType.DMA((z.tps * z.heads,))],
        places=[pltpu.HBM],
    )(out_weight)
    weights = exchange_all(sliced, "tp")
    slot_rows = pltpu.VMEM((z.slots, z.tokens, z.hd), bf16)
    strips = local_call(
        functools.partial(attend_kernel, z),
        [shape((z.part, z.out_tokens), bf16)] * z.ranks,
        scratch=[slot_rows, slot_rows, slot_rows]
        + [pltpu.VMEM((z.tokens, z.tokens), bf16), pltpu.VMEM((z.hd, z.out_tokens), bf16)],
        places=[pltpu.SMEM] + [pltpu.VMEM] * z.ranks,
        flops=4 * z.out_tokens * z.tokens * z.hd,
    )(block_mask.transpose(1, 2, 0), *parts)
    pieces = exchange_all(strips, "seq")

    def join(arrays):
        return local_call(
            functools.partial(join_kernel, z), [shape((z.ranks, z.part, z.out_tokens), bf16)]
        )(*arrays)[0]

    all_shape = (z.blocks, z.ranks, z.rows, z.cols)
    one_shape = (z.blocks, z.rows, z.cols)

    def project(sources, total, is_last):
        outs = [shape(all_shape, jnp.float32)]
        scratch = [pltpu.VMEM((len(sources), z.heads * z.part, z.tokens), bf16)]
        if is_last:
            outs = [shape(one_shape, jnp.float32)] + [shape(one_shape, bf16)] * (z.ranks - 1)
            scratch.append(pltpu.VMEM(all_shape, jnp.float32))
        return local_call(
            functools.partial(project_kernel, z, len(sources), total is not None, is_last),
            outs,
            scratch=scratch,
            flops=2 * len(sources) * z.heads * z.part * z.tokens * z.cols,
        )(
            *[tokens[t] for t in sources],
            *[weights[t] for t in sources],
            *([] if total is None else [total[0]]),
        )

    tokens = {0: join(pieces)}
    steps = [[0]]
    flip = z.tps // 2
    if flip:
        far = []
        for piece in pieces:
            far.append(exchange(piece, "tp", flip))
        tokens[flip] = join(far)
        steps.append([flip])
        flip //= 2
    while flip:
        for has in list(tokens):
            tokens[has ^ flip] = exchange(tokens[has], "tp", flip)
            steps.append([has ^ flip])
        flip //= 2
    sums = None
    if len(steps) == 4:
        steps = [steps[0], steps[1] + steps[2], steps[3]]
    for i, sources in enumerate(steps):
        sums = project(sources, sums, i == len(steps) - 1)
    got = exchange_all(sums, "seq")
    total = got[0]
    for term in got[1:]:
        total = total + term.astype(jnp.float32)
    return total.astype(bf16)


def body(queries, key_vectors, value_vectors, block_mask, out_weight):
    z = Sizes(
        lax.axis_size("seq"),
        lax.axis_size("tp"),
        queries.shape,
        block_mask.shape[0],
        out_weight.shape,
    )
    if not z.fits():
        return gathered_plan(queries, key_vectors, value_vectors, block_mask, out_weight)
    return stationary_plan(z, queries, key_vectors, value_vectors, block_mask, out_weight)


def solution(mesh):
    return jax.shard_map(
        body,
        mesh=mesh,
        in_specs=(
            P("groups", "seq", "tp"),
            P("groups", "seq", "tp"),
            P("groups", "seq", "tp"),
            P("tp", None, None),
            P("tp", "seq", None),
        ),
        out_specs=P("groups", "seq", "tp"),
        check_vma=False,
    )
```

```python
import functools
import math

import jax
import jax.numpy as jnp
import numpy as np
from jax import lax
from jax.experimental import pallas as pl
from jax.experimental.pallas import tpu as pltpu
from jax.sharding import PartitionSpec as P


KEYS = 28


def strip_tables(heads_local, blocks, slot_total):
    slot_ids = np.arange(slot_total)
    head_of = slot_ids * heads_local // slot_total
    per_head = np.bincount(head_of, minlength=heads_local)
    head_begin = np.cumsum(per_head) - per_head
    order_in_head = slot_ids - head_begin[head_of]
    head_share = per_head[head_of]
    first_block = order_in_head * blocks // head_share
    block_count = (order_in_head + 1) * blocks // head_share - first_block
    return (head_of, first_block, block_count)


def gathered_plan(queries, key_vectors, value_vectors, block_mask, out_weight):
    rank_count = lax.axis_size("seq")
    my_rank = lax.axis_index("seq")
    block_total, row_share, feature_width = queries.shape
    heads_local = block_mask.shape[0]
    head_size = feature_width // heads_local
    block_rows = row_share * rank_count
    per_rank = (heads_local + rank_count - 1) // rank_count
    slot_total = rank_count * per_rank
    least_share = slot_total // heads_local
    strip_cap = ((block_total + least_share - 1) // least_share + 1) // 2 * 2
    key_cap = min(KEYS, block_total)
    head_of, first_block, block_count = strip_tables(heads_local, block_total, slot_total)
    slot_grid = np.arange(slot_total).reshape(rank_count, per_rank).T
    paired = jnp.concatenate(
        [
            key_vectors.reshape(block_total, row_share, heads_local, head_size),
            value_vectors.reshape(block_total, row_share, heads_local, head_size),
        ],
        axis=3,
    )
    send_heads = jnp.asarray(head_of[slot_grid].reshape(-1), jnp.int32)
    chosen = jnp.take(paired, send_heads, axis=2)
    chosen = chosen.reshape(block_total, row_share, per_rank, rank_count, 2 * head_size)
    outgoing_pairs = chosen.transpose(2, 0, 3, 1, 4).reshape(
        per_rank, block_total, block_rows, 2 * head_size
    )
    flat_queries = queries.reshape(block_total, row_share, heads_local, head_size).transpose(
        0, 2, 1, 3
    )
    flat_queries = flat_queries.reshape(block_total * heads_local, row_share, head_size)
    positions = np.arange(strip_cap)
    unit_block = first_block[slot_grid][:, None, :] + positions[None, :, None]
    is_live = positions[None, :, None] < block_count[slot_grid][:, None, :]
    unit_index = np.where(is_live, unit_block * heads_local + head_of[slot_grid][:, None, :], 0)
    picked = jnp.take(flat_queries, jnp.asarray(unit_index.reshape(-1), jnp.int32), axis=0)
    picked = jnp.where(
        jnp.asarray(is_live.reshape(-1))[:, None, None], picked, jnp.zeros_like(picked)
    )
    outgoing_queries = picked.reshape(per_rank, strip_cap, block_rows, head_size)
    strip_queries, strip_pairs = (
        lax.all_to_all(outgoing_queries, "seq", split_axis=2, concat_axis=2, tiled=True),
        lax.all_to_all(outgoing_pairs, "seq", split_axis=2, concat_axis=2, tiled=True),
    )
    my_slots = my_rank * per_rank + jnp.arange(per_rank, dtype=jnp.int32)
    my_heads = jnp.asarray(head_of, jnp.int32)[my_slots]
    my_first = jnp.asarray(first_block, jnp.int32)[my_slots]
    query_blocks = jnp.minimum(
        my_first[:, None] + jnp.arange(strip_cap, dtype=jnp.int32)[None, :], block_total - 1
    )
    mask_rows = block_mask[my_heads[:, None], query_blocks]
    column_ids = jnp.arange(block_total, dtype=jnp.int32)
    ranking = (1 - mask_rows) * block_total + column_ids
    key_pick = jnp.argsort(ranking, axis=-1)[..., :key_cap]
    key_live = jnp.take_along_axis(mask_rows, key_pick, axis=-1)
    group_total = per_rank * strip_cap // 2
    query_groups = strip_queries.reshape(group_total, 2, block_rows, head_size)
    pick_groups = key_pick.reshape(group_total, 2, key_cap)
    live_groups = key_live.reshape(group_total, 2, key_cap)
    slot_of_group = jnp.arange(group_total, dtype=jnp.int32) // (strip_cap // 2)
    score_scale = head_size ** (-0.5)

    def attend_group(inputs):
        query_tile, pick_tile, live_tile, slot_index = inputs
        pairs_here = strip_pairs[slot_index]
        gathered = pairs_here[pick_tile]
        scores = (
            jnp.einsum(
                "qid,qkjd->qikj",
                query_tile,
                gathered[..., :head_size],
                preferred_element_type=jnp.float32,
            )
            * score_scale
        )
        allowed = (live_tile > 0)[:, None, :, None]
        scores = jnp.where(allowed, scores, -jnp.inf)
        largest = jnp.max(scores, axis=(2, 3), keepdims=True)
        weights = jnp.exp(scores - largest)
        totals = jnp.sum(weights, axis=(2, 3))
        blended = jnp.einsum(
            "qikj,qkjd->qid",
            weights.astype(jnp.bfloat16),
            gathered[..., head_size:],
            preferred_element_type=jnp.float32,
        )
        return (blended / totals[..., None]).astype(jnp.bfloat16)

    strip_out = lax.map(attend_group, (query_groups, pick_groups, live_groups, slot_of_group))
    outgoing_out = strip_out.reshape(per_rank, strip_cap, block_rows, head_size)
    returned = lax.all_to_all(outgoing_out, "seq", split_axis=2, concat_axis=2, tiled=True)
    slot_mesh, step_mesh = np.meshgrid(np.arange(slot_total), positions, indexing="ij")
    live_slot = step_mesh < block_count[slot_mesh]
    placement_index = np.zeros((block_total, heads_local), np.int64)
    source_index = (
        slot_mesh % per_rank * strip_cap + step_mesh
    ) * rank_count + slot_mesh // per_rank
    placement_index[
        first_block[slot_mesh][live_slot] + step_mesh[live_slot], head_of[slot_mesh][live_slot]
    ] = source_index[live_slot]
    flat_back = returned.reshape(per_rank * strip_cap * rank_count, row_share, head_size)
    own_out = jnp.take(flat_back, jnp.asarray(placement_index.reshape(-1), jnp.int32), axis=0)
    own_out = own_out.reshape(block_total, heads_local, row_share, head_size)
    token_total = block_total * row_share
    token_out = own_out.transpose(0, 2, 1, 3).reshape(token_total, heads_local, head_size)
    partial_sum = jnp.einsum(
        "thd,hdo->to",
        token_out,
        lax.all_gather(out_weight, "seq", axis=1, tiled=True),
        preferred_element_type=jnp.float32,
    )
    summed = lax.psum_scatter(
        partial_sum.astype(jnp.bfloat16), "tp", scatter_dimension=1, tiled=True
    ).astype(jnp.float32)
    return summed.astype(jnp.bfloat16).reshape(block_total, row_share, summed.shape[1])


def exchange(array, axis, flip):
    size = lax.axis_size(axis)
    return lax.ppermute(array, axis, [(i, i ^ flip) for i in range(size)])


def aligned(index, unit):
    return pl.multiple_of(index * unit, unit)


class Sizes:
    def __init__(self, rank_count, tp_count, queries_shape, heads_local, weight_shape):
        self.ranks = rank_count
        self.tps = tp_count
        self.blocks, self.rows, width = queries_shape
        self.heads = heads_local
        self.hd = width // heads_local
        self.whole = heads_local // rank_count
        self.rest = heads_local % rank_count
        self.sharers = rank_count // self.rest if self.rest else 1
        self.strip = self.blocks // self.sharers if self.rest else 0
        self.slots = self.whole + (1 if self.rest else 0)
        self.q_units = self.whole * self.blocks + self.strip
        self.kv_units = self.slots * self.blocks
        self.units = self.q_units + 2 * self.kv_units
        self.block_rows = self.rows * rank_count
        self.tokens = self.blocks * self.block_rows
        self.out_tokens = self.q_units * self.block_rows
        self.part = weight_shape[1]
        self.dout = weight_shape[2]
        self.cols = self.dout // tp_count

    def fits(self):
        power = lambda n: n & (n - 1) == 0
        if not (power(self.ranks) and power(self.tps) and self.whole > 0):
            return False
        if self.rest and (self.ranks % self.rest or self.blocks % self.sharers):
            return False
        if self.rows % 32 or self.part % 32 or self.hd % 128 or self.cols % 128:
            return False
        gathered = (self.ranks - 1) * self.heads * self.part * self.dout
        summed = (self.ranks - 1) * self.tokens // self.ranks * self.cols
        summed += (self.tps - 1) * self.heads * self.part * (self.cols + self.tokens)
        return summed < gathered


def run_copies(pairs, sems):
    copies = [pltpu.make_async_copy(a, b, sems.at[i]) for i, (a, b) in enumerate(pairs)]
    for copy in copies:
        copy.start()
    for copy in copies:
        copy.wait()


def pack_kernel(z, q_hbm, k_hbm, v_hbm, *refs):
    out_refs = refs[: z.ranks]
    q_ref, k_ref, v_ref, sems = refs[z.ranks :]
    me = lax.axis_index("seq")
    arrays = ((q_hbm, q_ref, 0), (k_hbm, k_ref, z.q_units), (v_hbm, v_ref, z.q_units + z.kv_units))
    copies = []
    for i, (hbm, ref, _) in enumerate(arrays):
        for b in range(z.blocks):
            copies.append(pltpu.make_async_copy(hbm.at[b], ref.at[b], sems.at[i * z.blocks + b]))
    for copy in copies:
        copy.start()
    for i, (_, ref, begin) in enumerate(arrays):
        for b in range(z.blocks):
            copies[i * z.blocks + b].wait()
            for flip in range(z.ranks):
                for slot in range(z.whole):
                    cols = pl.ds(aligned(slot * z.ranks + (me ^ flip), z.hd), z.hd)
                    out_refs[flip][begin + slot * z.blocks + b] = ref[b, :, cols]
        if z.rest:
            count = z.strip if i == 0 else z.blocks
            for flip in range(z.ranks):
                peer = me ^ flip
                cols = pl.ds(aligned(z.whole * z.ranks + peer // z.sharers, z.hd), z.hd)
                first = (peer % z.sharers) * z.strip if i == 0 else 0
                at = begin + z.whole * z.blocks
                out_refs[flip][at : at + count] = ref[pl.ds(first, count), :, cols]


def weight_kernel(z, w_hbm, *refs):
    out_refs, sems = refs[: z.tps], refs[z.tps]
    me = lax.axis_index("tp")
    pairs = []
    for head in range(z.heads):
        for flip in range(z.tps):
            cols = pl.ds(aligned(me ^ flip, z.cols), z.cols)
            pairs.append((w_hbm.at[head, :, cols], out_refs[flip].at[head]))
    run_copies(pairs, sems)


def attend_kernel(z, mask_ref, *refs):
    part_refs = refs[: z.ranks]
    out_refs = refs[z.ranks : 2 * z.ranks]
    query, keys, values, turned, raw, weights, result = refs[2 * z.ranks :]
    me = lax.axis_index("seq")
    scale = z.hd ** (-0.5) * math.log2(math.e)
    pairs = []
    for slot in range(z.slots):
        is_strip = slot >= z.whole
        count = z.strip if is_strip else z.blocks
        head = z.whole * z.ranks + me // z.sharers if is_strip else slot * z.ranks + me
        first = (me % z.sharers) * z.strip if is_strip else 0
        pairs.extend((slot, b, head, first + b) for b in range(count))
        for flip in range(z.ranks):
            for b in range(count):
                rows = pl.ds(b * z.block_rows + aligned(me ^ flip, z.rows), z.rows)
                query[slot, rows, :] = part_refs[flip][slot * z.blocks + b]
            for b in range(z.blocks):
                rows = pl.ds(b * z.block_rows + flip * z.rows, z.rows)
                unit = z.q_units + slot * z.blocks + b
                keys[slot, rows, :] = part_refs[flip][unit]
                values[slot, rows, :] = part_refs[flip][unit + z.kv_units]

    def score(i):
        slot, b, _, _ = pairs[i]
        raw[i % 2] = lax.dot_general(
            keys[slot],
            query[slot, b * z.block_rows : (b + 1) * z.block_rows, :],
            (((1,), (1,)), ((), ())),
            preferred_element_type=jnp.float32,
        )

    def weigh(i):
        _, _, head, block = pairs[i]
        spans = [slice(t * z.block_rows, (t + 1) * z.block_rows) for t in range(z.blocks)]
        allowed = [mask_ref[block, t, head] > 0 for t in range(z.blocks)]
        largest = None
        for span, live in zip(spans, allowed):
            peak = jnp.max(raw[i % 2, span].reshape(-1, 8, z.block_rows), axis=0)
            peak = jnp.where(live, peak, -jnp.inf)
            largest = peak if largest is None else jnp.maximum(largest, peak)
        largest = jnp.max(largest, axis=0, keepdims=True)
        total = None
        for span, live in zip(spans, allowed):
            exps = jnp.exp2((raw[i % 2, span] - jnp.where(live, largest, jnp.inf)) * scale)
            part = jnp.sum(exps.reshape(-1, 8, z.block_rows), axis=0)
            total = part if total is None else total + part
            weights[i % 2, span] = exps.astype(jnp.bfloat16)
        return jnp.sum(total, axis=0, keepdims=True)

    def blend(i, total):
        blended = jnp.dot(
            turned[pairs[i][0]], weights[i % 2], preferred_element_type=jnp.float32
        )
        lanes = slice(i * z.block_rows, (i + 1) * z.block_rows)
        result[:, lanes] = (blended / total).astype(jnp.bfloat16)

    score(0)
    for slot in range(z.slots):
        turned[slot] = values[slot].T
    total = None
    for i in range(len(pairs)):
        if i + 1 < len(pairs):
            score(i + 1)
        if i:
            blend(i - 1, total)
        total = weigh(i)
    blend(len(pairs) - 1, total)
    for flip in range(z.ranks):
        out_refs[flip][...] = result[pl.ds(aligned(me ^ flip, z.part), z.part), :]


def project_kernel(z, count, has_total, is_last, *refs):
    token_refs, refs = refs[: count * z.ranks], refs[count * z.ranks :]
    weight_refs, refs = refs[:count], refs[count:]
    if has_total:
        before, refs = refs[0], refs[1:]
    out_refs, inputs = refs[: z.ranks if is_last else 1], refs[z.ranks if is_last else 1]
    me = lax.axis_index("seq")
    acc = before[...].reshape(z.tokens, z.cols) if has_total else None
    for t in range(count):
        for flip in range(z.ranks):
            source = me ^ flip
            for slot in range(z.whole):
                rows = pl.ds(aligned(slot * z.ranks + source, z.part), z.part)
                lanes = slice(slot * z.tokens, (slot + 1) * z.tokens)
                inputs[t, rows, :] = token_refs[t * z.ranks + flip][:, lanes]
            if z.rest:
                head = z.whole * z.ranks + source // z.sharers
                wide = z.strip * z.block_rows
                at = pl.ds(aligned(source % z.sharers, wide), wide)
                lanes = slice(z.whole * z.tokens, z.whole * z.tokens + wide)
                inputs[t, pl.ds(aligned(head, z.part), z.part), at] = token_refs[t * z.ranks + flip][:, lanes]
    for t in range(count):
        w = weight_refs[t][...].reshape(z.heads * z.part, z.cols)
        term = lax.dot_general(
            inputs[t], w, (((0,), (0,)), ((), ())), preferred_element_type=jnp.float32
        )
        acc = term if acc is None else acc + term
    acc = acc.reshape(z.blocks, z.ranks, z.rows, z.cols)
    if not is_last:
        out_refs[0][...] = acc
        return
    total = refs[z.ranks + 1]
    total[...] = acc
    for b in range(z.blocks):
        out_refs[0][b] = total[b, me]
        for flip in range(1, z.ranks):
            out_refs[flip][b] = total[b, me ^ flip].astype(jnp.bfloat16)


def local_call(kernel, outs, scratch=(), places=None, limit=16, flops=1 << 20):
    def call(*args):
        spaces = places or [pltpu.VMEM] * len(args)
        args = [
            pltpu.with_memory_space_constraint(arg, space) if space is pltpu.HBM else arg
            for arg, space in zip(args, spaces)
        ]
        return pl.pallas_call(
            kernel,
            out_shape=outs,
            in_specs=[pl.BlockSpec(memory_space=space) for space in spaces],
            out_specs=[pl.BlockSpec(memory_space=pltpu.VMEM)] * len(outs),
            scratch_shapes=list(scratch),
            compiler_params=pltpu.CompilerParams(vmem_limit_bytes=limit << 20),
            cost_estimate=pl.CostEstimate(flops=flops, bytes_accessed=1 << 20, transcendentals=0),
        )(*args)

    return call


def exchange_all(arrays, axis):
    got = [arrays[0]]
    for flip in range(1, len(arrays)):
        got.append(exchange(arrays[flip], axis, flip))
    return got


def stationary_plan(z, queries, key_vectors, value_vectors, block_mask, out_weight):
    bf16 = jnp.bfloat16
    shape = jax.ShapeDtypeStruct
    packed = local_call(
        functools.partial(pack_kernel, z),
        [shape((z.units, z.rows, z.hd), bf16)] * z.ranks,
        scratch=[pltpu.VMEM(queries.shape, bf16)] * 3
        + [pltpu.SemaphoreType.DMA((3 * z.blocks,))],
        places=[pltpu.HBM] * 3,
    )(queries, key_vectors, value_vectors)
    parts = exchange_all(packed, "seq")
    sliced = local_call(
        functools.partial(weight_kernel, z),
        [shape((z.heads, z.part, z.cols), bf16)] * z.tps,
        scratch=[pltpu.SemaphoreType.DMA((z.tps * z.heads,))],
        places=[pltpu.HBM],
    )(out_weight)
    weights = exchange_all(sliced, "tp")
    slot_rows = pltpu.VMEM((z.slots, z.tokens, z.hd), bf16)
    strips = local_call(
        functools.partial(attend_kernel, z),
        [shape((z.part, z.out_tokens), bf16)] * z.ranks,
        scratch=[slot_rows, slot_rows, slot_rows]
        + [
            pltpu.VMEM((z.slots, z.hd, z.tokens), bf16),
            pltpu.VMEM((2, z.tokens, z.block_rows), jnp.float32),
            pltpu.VMEM((2, z.tokens, z.block_rows), bf16),
            pltpu.VMEM((z.hd, z.out_tokens), bf16),
        ],
        places=[pltpu.SMEM] + [pltpu.VMEM] * z.ranks,
        flops=4 * z.out_tokens * z.tokens * z.hd,
    )(block_mask.transpose(1, 2, 0), *parts)
    pieces = exchange_all(strips, "seq")

    all_shape = (z.blocks, z.ranks, z.rows, z.cols)
    one_shape = (z.blocks, z.rows, z.cols)

    def project(sources, total, is_last):
        outs = [shape(all_shape, jnp.float32)]
        scratch = [pltpu.VMEM((len(sources), z.heads * z.part, z.tokens), bf16)]
        if is_last:
            outs = [shape(one_shape, jnp.float32)] + [shape(one_shape, bf16)] * (z.ranks - 1)
            scratch.append(pltpu.VMEM(all_shape, jnp.float32))
        return local_call(
            functools.partial(project_kernel, z, len(sources), total is not None, is_last),
            outs,
            scratch=scratch,
            flops=2 * len(sources) * z.heads * z.part * z.tokens * z.cols,
        )(
            *[piece for t in sources for piece in tokens[t]],
            *[weights[t] for t in sources],
            *([] if total is None else [total[0]]),
        )

    tokens = {0: pieces}
    steps = [[0]]
    flip = z.tps // 2
    while flip:
        for has in list(tokens):
            tokens[has ^ flip] = []
            for piece in tokens[has]:
                tokens[has ^ flip].append(exchange(piece, "tp", flip))
            steps.append([has ^ flip])
        flip //= 2
    sums = None
    if len(steps) == 4:
        steps = [steps[0], steps[1] + steps[2], steps[3]]
    for i, sources in enumerate(steps):
        sums = project(sources, sums, i == len(steps) - 1)
    got = exchange_all(sums, "seq")
    total = got[0]
    for term in got[1:]:
        total = total + term.astype(jnp.float32)
    return total.astype(bf16)


def body(queries, key_vectors, value_vectors, block_mask, out_weight):
    z = Sizes(
        lax.axis_size("seq"),
        lax.axis_size("tp"),
        queries.shape,
        block_mask.shape[0],
        out_weight.shape,
    )
    if not z.fits():
        return gathered_plan(queries, key_vectors, value_vectors, block_mask, out_weight)
    return stationary_plan(z, queries, key_vectors, value_vectors, block_mask, out_weight)


def solution(mesh):
    return jax.shard_map(
        body,
        mesh=mesh,
        in_specs=(
            P("groups", "seq", "tp"),
            P("groups", "seq", "tp"),
            P("groups", "seq", "tp"),
            P("tp", None, None),
            P("tp", "seq", None),
        ),
        out_specs=P("groups", "seq", "tp"),
        check_vma=False,
    )
```

```python
import functools
import math

import jax
import jax.numpy as jnp
import numpy as np
from jax import lax
from jax.experimental import pallas as pl
from jax.experimental.pallas import tpu as pltpu
from jax.sharding import PartitionSpec as P


KEYS = 28


def strip_tables(heads_local, blocks, slot_total):
    slot_ids = np.arange(slot_total)
    head_of = slot_ids * heads_local // slot_total
    per_head = np.bincount(head_of, minlength=heads_local)
    head_begin = np.cumsum(per_head) - per_head
    order_in_head = slot_ids - head_begin[head_of]
    head_share = per_head[head_of]
    first_block = order_in_head * blocks // head_share
    block_count = (order_in_head + 1) * blocks // head_share - first_block
    return (head_of, first_block, block_count)


def gathered_plan(queries, key_vectors, value_vectors, block_mask, out_weight):
    rank_count = lax.axis_size("seq")
    my_rank = lax.axis_index("seq")
    block_total, row_share, feature_width = queries.shape
    heads_local = block_mask.shape[0]
    head_size = feature_width // heads_local
    block_rows = row_share * rank_count
    per_rank = (heads_local + rank_count - 1) // rank_count
    slot_total = rank_count * per_rank
    least_share = slot_total // heads_local
    strip_cap = ((block_total + least_share - 1) // least_share + 1) // 2 * 2
    key_cap = min(KEYS, block_total)
    head_of, first_block, block_count = strip_tables(heads_local, block_total, slot_total)
    slot_grid = np.arange(slot_total).reshape(rank_count, per_rank).T
    paired = jnp.concatenate(
        [
            key_vectors.reshape(block_total, row_share, heads_local, head_size),
            value_vectors.reshape(block_total, row_share, heads_local, head_size),
        ],
        axis=3,
    )
    send_heads = jnp.asarray(head_of[slot_grid].reshape(-1), jnp.int32)
    chosen = jnp.take(paired, send_heads, axis=2)
    chosen = chosen.reshape(block_total, row_share, per_rank, rank_count, 2 * head_size)
    outgoing_pairs = chosen.transpose(2, 0, 3, 1, 4).reshape(
        per_rank, block_total, block_rows, 2 * head_size
    )
    flat_queries = queries.reshape(block_total, row_share, heads_local, head_size).transpose(
        0, 2, 1, 3
    )
    flat_queries = flat_queries.reshape(block_total * heads_local, row_share, head_size)
    positions = np.arange(strip_cap)
    unit_block = first_block[slot_grid][:, None, :] + positions[None, :, None]
    is_live = positions[None, :, None] < block_count[slot_grid][:, None, :]
    unit_index = np.where(is_live, unit_block * heads_local + head_of[slot_grid][:, None, :], 0)
    picked = jnp.take(flat_queries, jnp.asarray(unit_index.reshape(-1), jnp.int32), axis=0)
    picked = jnp.where(
        jnp.asarray(is_live.reshape(-1))[:, None, None], picked, jnp.zeros_like(picked)
    )
    outgoing_queries = picked.reshape(per_rank, strip_cap, block_rows, head_size)
    strip_queries, strip_pairs = (
        lax.all_to_all(outgoing_queries, "seq", split_axis=2, concat_axis=2, tiled=True),
        lax.all_to_all(outgoing_pairs, "seq", split_axis=2, concat_axis=2, tiled=True),
    )
    my_slots = my_rank * per_rank + jnp.arange(per_rank, dtype=jnp.int32)
    my_heads = jnp.asarray(head_of, jnp.int32)[my_slots]
    my_first = jnp.asarray(first_block, jnp.int32)[my_slots]
    query_blocks = jnp.minimum(
        my_first[:, None] + jnp.arange(strip_cap, dtype=jnp.int32)[None, :], block_total - 1
    )
    mask_rows = block_mask[my_heads[:, None], query_blocks]
    column_ids = jnp.arange(block_total, dtype=jnp.int32)
    ranking = (1 - mask_rows) * block_total + column_ids
    key_pick = jnp.argsort(ranking, axis=-1)[..., :key_cap]
    key_live = jnp.take_along_axis(mask_rows, key_pick, axis=-1)
    group_total = per_rank * strip_cap // 2
    query_groups = strip_queries.reshape(group_total, 2, block_rows, head_size)
    pick_groups = key_pick.reshape(group_total, 2, key_cap)
    live_groups = key_live.reshape(group_total, 2, key_cap)
    slot_of_group = jnp.arange(group_total, dtype=jnp.int32) // (strip_cap // 2)
    score_scale = head_size ** (-0.5)

    def attend_group(inputs):
        query_tile, pick_tile, live_tile, slot_index = inputs
        pairs_here = strip_pairs[slot_index]
        gathered = pairs_here[pick_tile]
        scores = (
            jnp.einsum(
                "qid,qkjd->qikj",
                query_tile,
                gathered[..., :head_size],
                preferred_element_type=jnp.float32,
            )
            * score_scale
        )
        allowed = (live_tile > 0)[:, None, :, None]
        scores = jnp.where(allowed, scores, -jnp.inf)
        largest = jnp.max(scores, axis=(2, 3), keepdims=True)
        weights = jnp.exp(scores - largest)
        totals = jnp.sum(weights, axis=(2, 3))
        blended = jnp.einsum(
            "qikj,qkjd->qid",
            weights.astype(jnp.bfloat16),
            gathered[..., head_size:],
            preferred_element_type=jnp.float32,
        )
        return (blended / totals[..., None]).astype(jnp.bfloat16)

    strip_out = lax.map(attend_group, (query_groups, pick_groups, live_groups, slot_of_group))
    outgoing_out = strip_out.reshape(per_rank, strip_cap, block_rows, head_size)
    returned = lax.all_to_all(outgoing_out, "seq", split_axis=2, concat_axis=2, tiled=True)
    slot_mesh, step_mesh = np.meshgrid(np.arange(slot_total), positions, indexing="ij")
    live_slot = step_mesh < block_count[slot_mesh]
    placement_index = np.zeros((block_total, heads_local), np.int64)
    source_index = (
        slot_mesh % per_rank * strip_cap + step_mesh
    ) * rank_count + slot_mesh // per_rank
    placement_index[
        first_block[slot_mesh][live_slot] + step_mesh[live_slot], head_of[slot_mesh][live_slot]
    ] = source_index[live_slot]
    flat_back = returned.reshape(per_rank * strip_cap * rank_count, row_share, head_size)
    own_out = jnp.take(flat_back, jnp.asarray(placement_index.reshape(-1), jnp.int32), axis=0)
    own_out = own_out.reshape(block_total, heads_local, row_share, head_size)
    token_total = block_total * row_share
    token_out = own_out.transpose(0, 2, 1, 3).reshape(token_total, heads_local, head_size)
    partial_sum = jnp.einsum(
        "thd,hdo->to",
        token_out,
        lax.all_gather(out_weight, "seq", axis=1, tiled=True),
        preferred_element_type=jnp.float32,
    )
    summed = lax.psum_scatter(
        partial_sum.astype(jnp.bfloat16), "tp", scatter_dimension=1, tiled=True
    ).astype(jnp.float32)
    return summed.astype(jnp.bfloat16).reshape(block_total, row_share, summed.shape[1])


def exchange(array, axis, flip):
    size = lax.axis_size(axis)
    return lax.ppermute(array, axis, [(i, i ^ flip) for i in range(size)])


def aligned(index, unit):
    return pl.multiple_of(index * unit, unit)


class Sizes:
    def __init__(self, rank_count, tp_count, queries_shape, heads_local, weight_shape):
        self.ranks = rank_count
        self.tps = tp_count
        self.blocks, self.rows, width = queries_shape
        self.heads = heads_local
        self.hd = width // heads_local
        self.whole = heads_local // rank_count
        self.rest = heads_local % rank_count
        self.sharers = rank_count // self.rest if self.rest else 1
        self.strip = self.blocks // self.sharers if self.rest else 0
        self.slots = self.whole + (1 if self.rest else 0)
        self.q_units = self.whole * self.blocks + self.strip
        self.kv_units = self.slots * self.blocks
        self.units = self.q_units + 2 * self.kv_units
        self.block_rows = self.rows * rank_count
        self.tokens = self.blocks * self.block_rows
        self.out_tokens = self.q_units * self.block_rows
        self.part = weight_shape[1]
        self.dout = weight_shape[2]
        self.cols = self.dout // tp_count

    def fits(self):
        power = lambda n: n & (n - 1) == 0
        if not (power(self.ranks) and power(self.tps) and self.whole > 0):
            return False
        if self.rest and (self.ranks % self.rest or self.blocks % self.sharers):
            return False
        if self.rows % 32 or self.part % 32 or self.hd % 128 or self.cols % 128:
            return False
        gathered = (self.ranks - 1) * self.heads * self.part * self.dout
        summed = (self.ranks - 1) * self.tokens // self.ranks * self.cols
        summed += (self.tps - 1) * self.heads * self.part * (self.cols + self.tokens)
        return summed < gathered


def run_copies(pairs, sems):
    copies = [pltpu.make_async_copy(a, b, sems.at[i]) for i, (a, b) in enumerate(pairs)]
    for copy in copies:
        copy.start()
    for copy in copies:
        copy.wait()


def pack_kernel(z, flips, q_hbm, k_hbm, v_hbm, *refs):
    out_refs = dict(zip(flips, refs))
    q_ref, k_ref, v_ref, sems = refs[len(flips) :]
    me = lax.axis_index("seq")
    arrays = ((q_hbm, q_ref, 0), (k_hbm, k_ref, z.q_units), (v_hbm, v_ref, z.q_units + z.kv_units))
    copies = []
    for i, (hbm, ref, _) in enumerate(arrays):
        for b in range(z.blocks):
            copies.append(pltpu.make_async_copy(hbm.at[b], ref.at[b], sems.at[i * z.blocks + b]))
    for copy in copies:
        copy.start()
    for i, (_, ref, begin) in enumerate(arrays):
        for b in range(z.blocks):
            copies[i * z.blocks + b].wait()
            for flip in flips:
                for slot in range(z.whole):
                    cols = pl.ds(aligned(slot * z.ranks + (me ^ flip), z.hd), z.hd)
                    out_refs[flip][begin + slot * z.blocks + b] = ref[b, :, cols]
        if z.rest:
            count = z.strip if i == 0 else z.blocks
            for flip in flips:
                peer = me ^ flip
                cols = pl.ds(aligned(z.whole * z.ranks + peer // z.sharers, z.hd), z.hd)
                first = (peer % z.sharers) * z.strip if i == 0 else 0
                at = begin + z.whole * z.blocks
                out_refs[flip][at : at + count] = ref[pl.ds(first, count), :, cols]


def weight_kernel(z, w_hbm, *refs):
    out_refs, sems = refs[: z.tps], refs[z.tps]
    me = lax.axis_index("tp")
    pairs = []
    for head in range(z.heads):
        for flip in range(z.tps):
            cols = pl.ds(aligned(me ^ flip, z.cols), z.cols)
            pairs.append((w_hbm.at[head, :, cols], out_refs[flip].at[head]))
    run_copies(pairs, sems)


def attend_kernel(z, mask_ref, *refs):
    part_refs = refs[: z.ranks]
    out_refs = refs[z.ranks : 2 * z.ranks]
    query, keys, values, turned, raw, weights, result = refs[2 * z.ranks :]
    me = lax.axis_index("seq")
    scale = z.hd ** (-0.5) * math.log2(math.e)
    pairs = []
    for slot in range(z.slots):
        is_strip = slot >= z.whole
        count = z.strip if is_strip else z.blocks
        head = z.whole * z.ranks + me // z.sharers if is_strip else slot * z.ranks + me
        first = (me % z.sharers) * z.strip if is_strip else 0
        pairs.extend((slot, b, head, first + b) for b in range(count))
        for flip in range(z.ranks):
            for b in range(count):
                rows = pl.ds(b * z.block_rows + aligned(me ^ flip, z.rows), z.rows)
                query[slot, rows, :] = part_refs[flip][slot * z.blocks + b]
            for b in range(z.blocks):
                rows = pl.ds(b * z.block_rows + flip * z.rows, z.rows)
                unit = z.q_units + slot * z.blocks + b
                keys[slot, rows, :] = part_refs[flip][unit]
                values[slot, rows, :] = part_refs[flip][unit + z.kv_units]

    def score(i):
        slot, b, _, _ = pairs[i]
        raw[i % 2] = lax.dot_general(
            keys[slot],
            query[slot, b * z.block_rows : (b + 1) * z.block_rows, :],
            (((1,), (1,)), ((), ())),
            preferred_element_type=jnp.float32,
        )

    def weigh(i):
        _, _, head, block = pairs[i]
        spans = [slice(t * z.block_rows, (t + 1) * z.block_rows) for t in range(z.blocks)]
        allowed = [mask_ref[block, t, head] > 0 for t in range(z.blocks)]
        largest = None
        for span, live in zip(spans, allowed):
            peak = jnp.max(raw[i % 2, span].reshape(-1, 8, z.block_rows), axis=0)
            peak = jnp.where(live, peak, -jnp.inf)
            largest = peak if largest is None else jnp.maximum(largest, peak)
        largest = jnp.max(largest, axis=0, keepdims=True)
        total = None
        for span, live in zip(spans, allowed):
            exps = jnp.exp2((raw[i % 2, span] - jnp.where(live, largest, jnp.inf)) * scale)
            part = jnp.sum(exps.reshape(-1, 8, z.block_rows), axis=0)
            total = part if total is None else total + part
            weights[i % 2, span] = exps.astype(jnp.bfloat16)
        return jnp.sum(total, axis=0, keepdims=True)

    def blend(i, total):
        blended = jnp.dot(
            turned[pairs[i][0]], weights[i % 2], preferred_element_type=jnp.float32
        )
        lanes = slice(i * z.block_rows, (i + 1) * z.block_rows)
        result[:, lanes] = (blended / total).astype(jnp.bfloat16)

    score(0)
    for slot in range(z.slots):
        turned[slot] = values[slot].T
    total = None
    for i in range(len(pairs)):
        if i + 1 < len(pairs):
            score(i + 1)
        if i:
            blend(i - 1, total)
        total = weigh(i)
    blend(len(pairs) - 1, total)
    for flip in range(z.ranks):
        out_refs[flip][...] = result[pl.ds(aligned(me ^ flip, z.part), z.part), :]


def project_kernel(z, count, has_total, is_last, *refs):
    token_refs, refs = refs[: count * z.ranks], refs[count * z.ranks :]
    weight_refs, refs = refs[:count], refs[count:]
    if has_total:
        before, refs = refs[0], refs[1:]
    out_refs, inputs = refs[: z.ranks if is_last else 1], refs[z.ranks if is_last else 1]
    me = lax.axis_index("seq")
    acc = before[...].reshape(z.tokens, z.cols) if has_total else None
    for t in range(count):
        for flip in range(z.ranks):
            source = me ^ flip
            for slot in range(z.whole):
                rows = pl.ds(aligned(slot * z.ranks + source, z.part), z.part)
                lanes = slice(slot * z.tokens, (slot + 1) * z.tokens)
                inputs[t, rows, :] = token_refs[t * z.ranks + flip][:, lanes]
            if z.rest:
                head = z.whole * z.ranks + source // z.sharers
                wide = z.strip * z.block_rows
                at = pl.ds(aligned(source % z.sharers, wide), wide)
                lanes = slice(z.whole * z.tokens, z.whole * z.tokens + wide)
                inputs[t, pl.ds(aligned(head, z.part), z.part), at] = token_refs[t * z.ranks + flip][:, lanes]
    for t in range(count):
        w = weight_refs[t][...].reshape(z.heads * z.part, z.cols)
        term = lax.dot_general(
            inputs[t], w, (((0,), (0,)), ((), ())), preferred_element_type=jnp.float32
        )
        acc = term if acc is None else acc + term
    acc = acc.reshape(z.blocks, z.ranks, z.rows, z.cols)
    if not is_last:
        out_refs[0][...] = acc
        return
    total = refs[z.ranks + 1]
    total[...] = acc
    for b in range(z.blocks):
        out_refs[0][b] = total[b, me]
        for flip in range(1, z.ranks):
            out_refs[flip][b] = total[b, me ^ flip].astype(jnp.bfloat16)


def local_call(kernel, outs, scratch=(), places=None, limit=16, flops=1 << 20):
    def call(*args):
        spaces = places or [pltpu.VMEM] * len(args)
        args = [
            pltpu.with_memory_space_constraint(arg, space) if space is pltpu.HBM else arg
            for arg, space in zip(args, spaces)
        ]
        return pl.pallas_call(
            kernel,
            out_shape=outs,
            in_specs=[pl.BlockSpec(memory_space=space) for space in spaces],
            out_specs=[pl.BlockSpec(memory_space=pltpu.VMEM)] * len(outs),
            scratch_shapes=list(scratch),
            compiler_params=pltpu.CompilerParams(vmem_limit_bytes=limit << 20),
            cost_estimate=pl.CostEstimate(flops=flops, bytes_accessed=1 << 20, transcendentals=0),
        )(*args)

    return call


def exchange_all(arrays, axis):
    got = [arrays[0]]
    for flip in range(1, len(arrays)):
        got.append(exchange(arrays[flip], axis, flip))
    return got


def stationary_plan(z, queries, key_vectors, value_vectors, block_mask, out_weight):
    bf16 = jnp.bfloat16
    shape = jax.ShapeDtypeStruct

    def pack(flips):
        return local_call(
            functools.partial(pack_kernel, z, flips),
            [shape((z.units, z.rows, z.hd), bf16)] * len(flips),
            scratch=[pltpu.VMEM(queries.shape, bf16)] * 3
            + [pltpu.SemaphoreType.DMA((3 * z.blocks,))],
            places=[pltpu.HBM] * 3,
        )(queries, key_vectors, value_vectors)

    last = z.ranks - 1
    first_out = pack((last,))
    packed = list(pack(tuple(range(last)))) + list(first_out)
    parts = exchange_all(packed, "seq")
    sliced = local_call(
        functools.partial(weight_kernel, z),
        [shape((z.heads, z.part, z.cols), bf16)] * z.tps,
        scratch=[pltpu.SemaphoreType.DMA((z.tps * z.heads,))],
        places=[pltpu.HBM],
    )(out_weight)
    weights = exchange_all(sliced, "tp")
    slot_rows = pltpu.VMEM((z.slots, z.tokens, z.hd), bf16)
    strips = local_call(
        functools.partial(attend_kernel, z),
        [shape((z.part, z.out_tokens), bf16)] * z.ranks,
        scratch=[slot_rows, slot_rows, slot_rows]
        + [
            pltpu.VMEM((z.slots, z.hd, z.tokens), bf16),
            pltpu.VMEM((2, z.tokens, z.block_rows), jnp.float32),
            pltpu.VMEM((2, z.tokens, z.block_rows), bf16),
            pltpu.VMEM((z.hd, z.out_tokens), bf16),
        ],
        places=[pltpu.SMEM] + [pltpu.VMEM] * z.ranks,
        flops=4 * z.out_tokens * z.tokens * z.hd,
    )(block_mask.transpose(1, 2, 0), *parts)
    pieces = exchange_all(strips, "seq")

    all_shape = (z.blocks, z.ranks, z.rows, z.cols)
    one_shape = (z.blocks, z.rows, z.cols)

    def project(sources, total, is_last):
        outs = [shape(all_shape, jnp.float32)]
        scratch = [pltpu.VMEM((len(sources), z.heads * z.part, z.tokens), bf16)]
        if is_last:
            outs = [shape(one_shape, jnp.float32)] + [shape(one_shape, bf16)] * (z.ranks - 1)
            scratch.append(pltpu.VMEM(all_shape, jnp.float32))
        return local_call(
            functools.partial(project_kernel, z, len(sources), total is not None, is_last),
            outs,
            scratch=scratch,
            flops=2 * len(sources) * z.heads * z.part * z.tokens * z.cols,
        )(
            *[piece for t in sources for piece in tokens[t]],
            *[weights[t] for t in sources],
            *([] if total is None else [total[0]]),
        )

    tokens = {0: pieces}
    steps = [[0]]
    flip = z.tps // 2
    while flip:
        for has in list(tokens):
            tokens[has ^ flip] = []
            for piece in tokens[has]:
                tokens[has ^ flip].append(exchange(piece, "tp", flip))
            steps.append([has ^ flip])
        flip //= 2
    sums = None
    if len(steps) == 4:
        steps = [steps[0], steps[1] + steps[2], steps[3]]
    for i, sources in enumerate(steps):
        sums = project(sources, sums, i == len(steps) - 1)
    got = exchange_all(sums, "seq")
    total = got[0]
    for term in got[1:]:
        total = total + term.astype(jnp.float32)
    return total.astype(bf16)


def body(queries, key_vectors, value_vectors, block_mask, out_weight):
    z = Sizes(
        lax.axis_size("seq"),
        lax.axis_size("tp"),
        queries.shape,
        block_mask.shape[0],
        out_weight.shape,
    )
    if not z.fits():
        return gathered_plan(queries, key_vectors, value_vectors, block_mask, out_weight)
    return stationary_plan(z, queries, key_vectors, value_vectors, block_mask, out_weight)


def solution(mesh):
    return jax.shard_map(
        body,
        mesh=mesh,
        in_specs=(
            P("groups", "seq", "tp"),
            P("groups", "seq", "tp"),
            P("groups", "seq", "tp"),
            P("tp", None, None),
            P("tp", "seq", None),
        ),
        out_specs=P("groups", "seq", "tp"),
        check_vma=False,
    )
```
